256 devices in a mesh: dom: 32 (over x, z), rows: 8 (over y, core).
Axes of the slice: x: 4, y: 4, z: 8, core: 2. Of those that a mesh axis runs over, the one named last changes fastest.
Arguments:
- features: bfloat16 [65536, 384], P(('dom', 'rows')), may hold values from -7 to 7
- out_grad: bfloat16 [65536, 384], P(('dom', 'rows')), may hold values from -6 to 6
- w_query: bfloat16 [384, 384], replicated, may hold values from -0.3125 to 0.3125
- w_keyval: bfloat16 [384, 768], replicated, may hold values from -0.3125 to 0.3125
- w_out: bfloat16 [384, 384], replicated, may hold values from -0.3125 to 0.3125
- virtual: bfloat16 [4, 384], replicated, may hold values from -6 to 6
- local_nbr: int32 [65536, 16], P(('dom', 'rows')), may hold values from 0 to 255
- expander: int32 [65536, 4], P(('dom', 'rows')), may hold values from 0 to 1023
- send_rows: int32 [8192, 32], P(('dom', 'rows')), may hold values from 0 to 255
Outputs:
- grad_features: float32 [65536, 384], P(('dom', 'rows'))
- grad_wq: float32 [384, 384], replicated
- grad_wkv: float32 [384, 768], replicated
- grad_wo: float32 [384, 384], replicated
- grad_virtual: float32 [4, 384], replicated
The draws below stay inside these ranges and needn't reach their ends.
Inputs may be any that keep to these rules, and one draw needn't show every extreme that they name: `local_nbr`: positions 0 to 127 name the previous tile of the partition's block order (cyclic within the partition), 128 to 255 the node's own tile. `expander`: slot s * 32 + k of a device holds the k-th row that the device of dom index s and the same rows index sends to it. `send_rows`: row g * 32 + a lists the 32 local rows that device g sends to dom index a; every device sends exactly 32 rows to every dom index, itself included.
All inputs are finite; a program needn't handle non-finite values.
Results may differ from the reference program's by a relative error of at most 0.008.
The reference program's roundings to bfloat16 on the way count: a program that leaves them out, or rounds other values in their place, can miss the bound.
Values may be sent and summed in bfloat16 or wider, within the bound.
A program may use at most 64 MiB of HBM per device.

```python
import math
import jax
import jax.numpy as jnp
from jax import lax

D = 384
HEADS = 8
VIRTUAL = 4
EXP_DEG = 4
LOCAL = 16
TILE = 128
ROWS_DEV = 256
SLOTS_PEER = 32
NODES = 65536
SLOTS = 1024
SEND_LISTS = 8192
N_DOM = 32
N_ROWS = 8


def draw_features(key, part):
    base_key = jax.random.fold_in(key, 0)
    values = jax.random.truncated_normal(base_key, -6.0, 6.0, (NODES, D), jnp.float32)
    return values.astype(jnp.bfloat16)


def set_ends(entries, stream_key, least, largest):
    place = [jax.random.randint(jax.random.fold_in(stream_key, axis), (), 0, length) for axis, length in enumerate(entries.shape)]
    main_axis = entries.shape.index(max(entries.shape))
    beside = place[:main_axis] + [(place[main_axis] + 1) % entries.shape[main_axis]] + place[main_axis + 1:]
    return entries.at[tuple(place)].set(least).at[tuple(beside)].set(largest)


def level_of(own_key, extent, pieces, low, largest):
    def one(axis_at, shards_of):
        heights = jax.random.uniform(jax.random.fold_in(jax.random.fold_in(own_key, 6), axis_at), (shards_of,), jnp.float32, low / len(pieces), largest / len(pieces))
        return jnp.repeat(jnp.exp(heights), extent[axis_at] // shards_of).reshape((-1,) + (1,) * (len(extent) - axis_at - 1))

    level = one(*pieces[0])
    for cut in pieces[1:]:
        level = level * one(*cut)
    return level


def bell_draw(rng, dims, deviation, limit, cuts=(), held_as=jnp.bfloat16):
    level = level_of(rng, dims, cuts, -0.22, 0.18) if cuts else 1.0
    drawn = jax.random.normal(rng, dims, jnp.float32) * deviation * level
    return jnp.minimum(jnp.maximum(drawn, -limit), limit).astype(held_as)


def setup_inputs(seed: int = 0) -> dict:
    keys = jax.random.split(jax.random.key(seed), 10)
    features = draw_features(jax.random.fold_in(keys[9], 71), 0)
    out_grad = bell_draw(keys[1], (NODES, D), 1.0, 6.0, ((0, 256),))
    w_query = bell_draw(keys[2], (D, D), D ** -0.5, 0.3125)
    w_keyval = bell_draw(keys[3], (D, 2 * D), D ** -0.5, 0.3125)
    w_out = bell_draw(keys[4], (D, D), D ** -0.5, 0.3125)
    virtual = bell_draw(keys[5], (VIRTUAL, D), 1.0, 6.0)
    local_nbr = set_ends(jax.random.randint(keys[6], (NODES, LOCAL), 0, 2 * TILE), jax.random.fold_in(keys[6], 1), 0, (2 * TILE) - 1).astype(jnp.int32)
    expander = set_ends(jax.random.randint(keys[7], (NODES, EXP_DEG), 0, SLOTS), jax.random.fold_in(keys[7], 1), 0, SLOTS - 1).astype(jnp.int32)
    send_rows = set_ends(jax.random.randint(keys[8], (SEND_LISTS, SLOTS_PEER), 0, ROWS_DEV), jax.random.fold_in(keys[8], 1), 0, ROWS_DEV - 1).astype(jnp.int32)
    return dict(features=features, out_grad=out_grad, w_query=w_query, w_keyval=w_keyval, w_out=w_out, virtual=virtual, local_nbr=local_nbr, expander=expander, send_rows=send_rows)


NEGATIVE_FILL = -1e+30

def einsum_f32(spec, left, right):
    return jnp.einsum(spec, left.astype(jnp.float32), right.astype(jnp.float32))

def attend(queries, key_value, halo_kv, expand_kv, virtual_kv, local_nbr, out_delta):
    row_count, feat_width = queries.shape
    head_count = HEADS
    head_dim = feat_width // head_count
    tile_rows = TILE
    tile_count = row_count // tile_rows
    score_scale = 1.0 / math.sqrt(head_dim)
    extended = jnp.concatenate([halo_kv, key_value], axis=0)
    window = jnp.concatenate([extended[:row_count].reshape(tile_count, tile_rows, 2 * feat_width), key_value.reshape(tile_count, tile_rows, 2 * feat_width)], axis=1)
    win_keys = window[:, :, :feat_width].reshape(tile_count, 2 * tile_rows, head_count, head_dim)
    win_vals = window[:, :, feat_width:].reshape(tile_count, 2 * tile_rows, head_count, head_dim)
    exp_keys = expand_kv[:, :, :feat_width].reshape(row_count, -1, head_count, head_dim)
    exp_vals = expand_kv[:, :, feat_width:].reshape(row_count, -1, head_count, head_dim)
    virt_keys = virtual_kv[:, :feat_width].reshape(-1, head_count, head_dim)
    virt_vals = virtual_kv[:, feat_width:].reshape(-1, head_count, head_dim)
    q_heads = queries.reshape(row_count, head_count, head_dim)
    q_tiles = queries.reshape(tile_count, tile_rows, head_count, head_dim)
    d_heads = out_delta.reshape(row_count, head_count, head_dim)
    d_tiles = out_delta.reshape(tile_count, tile_rows, head_count, head_dim)
    positions = jnp.arange(2 * tile_rows, dtype=jnp.int32)
    local_mask = jnp.any(local_nbr[:, :, None] == positions[None, None, :], axis=1)[:, None, :]
    s_loc = einsum_f32('tqhd,tkhd->tqhk', q_tiles, win_keys).reshape(row_count, head_count, 2 * tile_rows) * score_scale
    s_loc = jnp.where(local_mask, s_loc, NEGATIVE_FILL)
    s_exp = einsum_f32('rhd,rkhd->rhk', q_heads, exp_keys) * score_scale
    s_virt = einsum_f32('rhd,khd->rhk', q_heads, virt_keys) * score_scale
    row_peak = jnp.maximum(jnp.maximum(s_loc.max(-1), s_exp.max(-1)), s_virt.max(-1))[..., None]
    e_loc = jnp.where(local_mask, jnp.exp(s_loc - row_peak), 0.0)
    e_exp = jnp.exp(s_exp - row_peak)
    e_virt = jnp.exp(s_virt - row_peak)
    norm_total = (e_loc.sum(-1) + e_exp.sum(-1) + e_virt.sum(-1))[..., None]
    p_loc = e_loc / norm_total
    p_exp = e_exp / norm_total
    p_virt = e_virt / norm_total
    pb_loc = p_loc.astype(jnp.bfloat16)
    pb_exp = p_exp.astype(jnp.bfloat16)
    pb_virt = p_virt.astype(jnp.bfloat16)
    pb_tiles = pb_loc.reshape(tile_count, tile_rows, head_count, 2 * tile_rows)
    summed = einsum_f32('tqhk,tkhd->tqhd', pb_tiles, win_vals).reshape(row_count, feat_width) + einsum_f32('rhk,rkhd->rhd', pb_exp, exp_vals).reshape(row_count, feat_width) + einsum_f32('rhk,khd->rhd', pb_virt, virt_vals).reshape(row_count, feat_width)
    attn_out = summed.astype(jnp.bfloat16)
    dp_loc = einsum_f32('tqhd,tkhd->tqhk', d_tiles, win_vals).reshape(row_count, head_count, 2 * tile_rows)
    dp_exp = einsum_f32('rhd,rkhd->rhk', d_heads, exp_vals)
    dp_virt = einsum_f32('rhd,khd->rhk', d_heads, virt_vals)
    delta = ((p_loc * dp_loc).sum(-1) + (p_exp * dp_exp).sum(-1) + (p_virt * dp_virt).sum(-1))[..., None]
    ds_loc = (p_loc * (dp_loc - delta) * score_scale).astype(jnp.bfloat16)
    ds_exp = (p_exp * (dp_exp - delta) * score_scale).astype(jnp.bfloat16)
    ds_virt = (p_virt * (dp_virt - delta) * score_scale).astype(jnp.bfloat16)
    ds_tiles = ds_loc.reshape(tile_count, tile_rows, head_count, 2 * tile_rows)
    grad_query = (einsum_f32('tqhk,tkhd->tqhd', ds_tiles, win_keys).reshape(row_count, feat_width) + einsum_f32('rhk,rkhd->rhd', ds_exp, exp_keys).reshape(row_count, feat_width) + einsum_f32('rhk,khd->rhd', ds_virt, virt_keys).reshape(row_count, feat_width)).astype(jnp.bfloat16)
    win_kgrad = einsum_f32('tqhk,tqhd->tkhd', ds_tiles, q_tiles).reshape(tile_count, 2 * tile_rows, feat_width)
    win_vgrad = einsum_f32('tqhk,tqhd->tkhd', pb_tiles, d_tiles).reshape(tile_count, 2 * tile_rows, feat_width)
    window_grad = jnp.concatenate([win_kgrad, win_vgrad], axis=-1)
    exp_grad = jnp.concatenate([einsum_f32('rhk,rhd->rkhd', ds_exp, q_heads).reshape(row_count, -1, feat_width), einsum_f32('rhk,rhd->rkhd', pb_exp, d_heads).reshape(row_count, -1, feat_width)], axis=-1)
    virt_grad = jnp.concatenate([einsum_f32('rhk,rhd->khd', ds_virt, q_heads).reshape(-1, feat_width), einsum_f32('rhk,rhd->khd', pb_virt, d_heads).reshape(-1, feat_width)], axis=-1)
    return (attn_out, grad_query, window_grad, exp_grad, virt_grad)

def rows_contracted(left, right):
    return lax.dot_general(left, right, (((0,), (0,)), ((), ())), preferred_element_type=jnp.float32)

def times_transposed(left, right):
    return lax.dot_general(left, right, (((1,), (1,)), ((), ())), preferred_element_type=jnp.float32)

def reference(features, out_grad, w_query, w_keyval, w_out, virtual, local_nbr, expander, send_rows):
    device_count = N_DOM * N_ROWS
    row_count = ROWS_DEV
    feat_width = D
    tile_rows = TILE
    queries = jnp.dot(features, w_query, preferred_element_type=jnp.float32).astype(jnp.bfloat16)
    key_value = jnp.dot(features, w_keyval, preferred_element_type=jnp.float32).astype(jnp.bfloat16)
    virtual_kv = jnp.dot(virtual, w_keyval, preferred_element_type=jnp.float32).astype(jnp.bfloat16)
    out_delta = times_transposed(out_grad, w_out).astype(jnp.bfloat16)
    device_ids = jnp.arange(device_count, dtype=jnp.int32)
    dom_of = device_ids // N_ROWS
    row_of = device_ids % N_ROWS
    previous = dom_of * N_ROWS + (row_of - 1) % N_ROWS
    following = dom_of * N_ROWS + (row_of + 1) % N_ROWS
    kv_dev = key_value.reshape(device_count, row_count, 2 * feat_width)
    halo_all = kv_dev[previous, row_count - tile_rows:]
    send_all = send_rows.reshape(device_count, N_DOM, SLOTS_PEER)
    sources = jnp.arange(N_DOM, dtype=jnp.int32)[None, :] * N_ROWS + row_of[:, None]
    picked = send_all[sources, dom_of[:, None], :]
    slot_nodes = (sources[:, :, None] * row_count + picked).reshape(device_count, N_DOM * SLOTS_PEER).astype(jnp.int32)

    def per_device(inputs):
        q_dev, kv_here, halo_kv, nodes_here, local_here, expand_here, delta_here = inputs
        slot_kv = key_value[nodes_here]
        expand_kv = slot_kv[expand_here]
        attn_out, grad_query, window_grad, exp_grad, virt_grad = attend(q_dev, kv_here, halo_kv, expand_kv, virtual_kv, local_here, delta_here)
        own_grad = window_grad[:, tile_rows:].reshape(row_count, 2 * feat_width)
        prev_grad = window_grad[:, :tile_rows].reshape(row_count, 2 * feat_width)
        partial_grad = own_grad + jnp.concatenate([prev_grad[tile_rows:], jnp.zeros((tile_rows, 2 * feat_width), jnp.float32)], axis=0)
        slot_grad = jax.ops.segment_sum(exp_grad.reshape(-1, 2 * feat_width), expand_here.reshape(-1), num_segments=nodes_here.shape[0]).astype(jnp.bfloat16)
        return (attn_out, grad_query, partial_grad, prev_grad[:tile_rows], slot_grad, virt_grad)
    attn_out, grad_query, partial_grad, halo_grad, slot_grad, virt_grad = lax.map(per_device, (queries.reshape(device_count, row_count, feat_width), kv_dev, halo_all, slot_nodes, local_nbr.reshape(device_count, row_count, LOCAL), expander.reshape(device_count, row_count, EXP_DEG), out_delta.reshape(device_count, row_count, feat_width)))
    returned = halo_grad[following]
    local_grad = partial_grad + jnp.concatenate([jnp.zeros((device_count, row_count - tile_rows, 2 * feat_width), jnp.float32), returned], axis=1)
    local_grad = local_grad.reshape(-1, 2 * feat_width).astype(jnp.bfloat16)
    grad_query = grad_query.reshape(-1, feat_width)
    attn_out = attn_out.reshape(-1, feat_width)
    slot_flat = slot_grad.reshape(-1, 2 * feat_width)
    nodes_flat = slot_nodes.reshape(-1)
    slot_feat = lax.optimization_barrier(times_transposed(slot_flat, w_keyval).astype(jnp.bfloat16))
    grad_features = times_transposed(grad_query, w_query) + times_transposed(local_grad, w_keyval)
    grad_features = grad_features.at[nodes_flat].add(slot_feat.astype(jnp.float32))
    virt_total = lax.optimization_barrier(jnp.sum(virt_grad, axis=0))
    factor = NODES ** (-0.5)
    grad_wq = rows_contracted(features, grad_query)
    grad_wkv = rows_contracted(features, local_grad) + rows_contracted(features[nodes_flat], slot_flat)
    grad_wkv = grad_wkv + jnp.dot(virtual.astype(jnp.float32).T, virt_total, precision=lax.Precision.HIGHEST)
    grad_wo = rows_contracted(attn_out, out_grad)
    grad_virtual = jnp.dot(virt_total, w_keyval.astype(jnp.float32).T, precision=lax.Precision.HIGHEST)
    return (grad_features, grad_wq * factor, grad_wkv * factor, grad_wo * factor, grad_virtual * factor)
```

```python
import functools
import math

import jax
import jax.numpy as jnp
from jax import lax
from jax.experimental import pallas as pl
from jax.experimental.pallas import tpu as pltpu
from jax.sharding import PartitionSpec as P

HEADS = 8
TILE = 128
LANES = 128
VROWS = 16
NEGATIVE_FILL = -1e30

F32 = jnp.float32
BF16 = jnp.bfloat16
VMEM = pl.BlockSpec(memory_space=pltpu.VMEM)


def contract(left, right, left_dim, right_dim):
    return lax.dot_general(
        left, right, (((left_dim,), (right_dim,)), ((), ())), preferred_element_type=F32
    )


def row_picker(send_flat, row_count):
    rows = lax.broadcasted_iota(jnp.int32, (row_count, send_flat.shape[1]), 0)
    return (rows == send_flat).astype(F32).astype(BF16)


def remote(src, dst, send_sem, recv_sem, dom, row):
    return pltpu.make_async_remote_copy(
        src_ref=src,
        dst_ref=dst,
        send_sem=send_sem,
        recv_sem=recv_sem,
        device_id=(dom, row),
        device_id_type=pl.DeviceIdType.MESH,
    )


def greet(n_dom, n_rows):
    dom, row = lax.axis_index("dom"), lax.axis_index("rows")
    barrier = pltpu.get_barrier_semaphore()

    def dom_peer(step, carry):
        pl.semaphore_signal(
            barrier,
            inc=1,
            device_id=(lax.rem(dom + step, n_dom), row),
            device_id_type=pl.DeviceIdType.MESH,
        )
        return carry

    def row_peer(step, carry):
        pl.semaphore_signal(
            barrier,
            inc=1,
            device_id=(dom, lax.rem(row + step, n_rows)),
            device_id_type=pl.DeviceIdType.MESH,
        )
        return carry

    lax.fori_loop(1, n_dom, dom_peer, 0)
    lax.fori_loop(1, n_rows, row_peer, 0)
    return barrier, n_dom + n_rows - 2


def spread_kernel(
    n_dom, n_rows, send_flat, feat, slots, halo, picked, send_sem, recv_sem, halo_send, halo_recv
):
    dom, row = lax.axis_index("dom"), lax.axis_index("rows")
    barrier, arrivals = greet(n_dom, n_rows)
    row_count, width = feat.shape
    picker = row_picker(send_flat[...], row_count)
    picked[...] = contract(picker, feat[...], 0, 0).astype(BF16).reshape(picked.shape)
    pl.semaphore_wait(barrier, arrivals)

    following = lax.rem(row + 1, n_rows)
    halo_copy = remote(
        feat.at[pl.ds(row_count - TILE, TILE)], halo, halo_send, halo_recv, dom, following
    )
    halo_copy.start()

    def copy_of(step):
        peer = lax.rem(dom + step, n_dom)
        return remote(
            picked.at[peer], slots.at[dom], send_sem.at[step], recv_sem.at[step], peer, row
        )

    def start(step, carry):
        copy_of(step).start()
        return carry

    def finish(step, carry):
        copy_of(step).wait()
        return carry

    lax.fori_loop(1, n_dom, start, 0)
    slots[dom] = picked[dom]
    halo_copy.wait()
    lax.fori_loop(1, n_dom, finish, 0)


def attend_kernel(
    feat,
    halo,
    slotf,
    out_grad,
    w_query,
    w_keyval,
    w_out,
    virt,
    local_nbr,
    expander,
    slot_feat,
    halo_feat,
    weight_sums,
    virt_feat,
    grad_feat,
    ext,
    q_t,
    d_t,
    kv_t,
    slot_kv,
    named,
    edge_kv,
    bias,
    edge_s,
    edge_dp,
    edge_p,
    edge_ds,
    kv_grad,
    out_t,
    dq_t,
    edge_grad,
):
    row_count, width = feat.shape
    slot_count = slotf.shape[0]
    head_dim = width // HEADS
    degree = expander.shape[0]
    scale = 1.0 / math.sqrt(head_dim)
    tiles = row_count // TILE

    ext[0:TILE] = halo[...]
    ext[TILE:] = feat[...]
    q_t[...] = contract(w_query[...], feat[...], 0, 1).astype(BF16)
    d_t[...] = contract(w_out[...], out_grad[...], 1, 1).astype(BF16)
    kv_t[...] = contract(w_keyval[...], ext[...], 0, 1).astype(BF16)
    virt_kv = contract(w_keyval[...], virt[...], 0, 1).astype(BF16).astype(F32)
    slot_kv[...] = contract(w_keyval[...], slotf[...], 0, 1).astype(BF16)

    positions = lax.broadcasted_iota(jnp.int32, (2 * TILE, row_count), 0)
    mask = positions == local_nbr[0:1, :]
    for entry in range(1, local_nbr.shape[0]):
        mask = jnp.logical_or(mask, positions == local_nbr[entry : entry + 1, :])
    bias[...] = jnp.where(mask, 0.0, NEGATIVE_FILL)

    slot_ids = lax.broadcasted_iota(jnp.int32, (slot_count, row_count), 0)
    q_wide = q_t[...].astype(F32)
    d_wide = d_t[...].astype(F32)

    def per_head(product):
        return product.reshape(HEADS, head_dim, row_count).sum(axis=1)

    def virtual_edge(v):
        return jnp.broadcast_to(virt_kv[:, v : v + 1], (2 * width, row_count))

    for k in range(degree):
        hot = (slot_ids == expander[k : k + 1, :]).astype(F32).astype(BF16)
        named[:, k * row_count : (k + 1) * row_count] = hot
        edge_kv[k] = contract(slot_kv[...], hot, 1, 0).astype(BF16)
        edge_s[:, k, :] = per_head(q_wide * edge_kv[k, 0:width].astype(F32)) * scale
        edge_dp[:, k, :] = per_head(d_wide * edge_kv[k, width:].astype(F32))
    for v in range(4):
        both = virtual_edge(v)
        edge_s[:, degree + v, :] = per_head(q_wide * both[0:width]) * scale
        edge_dp[:, degree + v, :] = per_head(d_wide * both[width:])

    kv_grad[...] = jnp.zeros_like(kv_grad)
    for h in range(HEADS):
        own = slice(h * head_dim, (h + 1) * head_dim)
        val = slice(width + h * head_dim, width + (h + 1) * head_dim)
        for t in range(tiles):
            here = slice(t * TILE, (t + 1) * TILE)
            window = slice(t * TILE, (t + 2) * TILE)
            keys, values = kv_t[own, window], kv_t[val, window]
            q_h, d_h = q_t[own, here], d_t[own, here]
            s = contract(keys, q_h, 0, 0) * scale + bias[:, here]
            se = edge_s[h, :, here]
            peak = jnp.maximum(
                jnp.max(s, axis=0, keepdims=True), jnp.max(se, axis=0, keepdims=True)
            )
            e = jnp.exp(s - peak)
            ee = jnp.exp(se - peak)
            inverse = 1.0 / (
                jnp.sum(e, axis=0, keepdims=True) + jnp.sum(ee, axis=0, keepdims=True)
            )
            p = e * inverse
            pe = ee * inverse
            dp = contract(values, d_h, 0, 0)
            dpe = edge_dp[h, :, here]
            delta = jnp.sum(p * dp, axis=0, keepdims=True) + jnp.sum(
                pe * dpe, axis=0, keepdims=True
            )
            ds = (p * (dp - delta) * scale).astype(BF16)
            pb = p.astype(BF16)
            edge_p[h, :, here] = pe.astype(BF16).astype(F32)
            edge_ds[h, :, here] = (pe * (dpe - delta) * scale).astype(BF16).astype(F32)
            out_t[own, here] = contract(values, pb, 1, 0)
            dq_t[own, here] = contract(keys, ds, 1, 0)
            kv_grad[own, window] += contract(q_h, ds, 1, 1)
            kv_grad[val, window] += contract(d_h, pb, 1, 1)

    def widen(rows):
        return jnp.broadcast_to(rows[:, None, :], (HEADS, head_dim, row_count)).reshape(
            width, row_count
        )

    out_sum = out_t[...]
    dq_sum = dq_t[...]
    lane = lax.broadcasted_iota(jnp.int32, (2 * width, LANES), 1)
    virt_t = jnp.zeros((2 * width, LANES), F32)
    for k in range(degree + 4):
        pk, dsk = widen(edge_p[:, k, :]), widen(edge_ds[:, k, :])
        if k < degree:
            key_k, val_k = edge_kv[k, 0:width].astype(F32), edge_kv[k, width:].astype(F32)
        else:
            both = virtual_edge(k - degree)
            key_k, val_k = both[0:width], both[width:]
        out_sum = out_sum + pk * val_k
        dq_sum = dq_sum + dsk * key_k
        to_key, to_val = dsk * q_wide, pk * d_wide
        if k < degree:
            cols = slice(k * row_count, (k + 1) * row_count)
            edge_grad[0:width, cols] = to_key.astype(BF16)
            edge_grad[width:, cols] = to_val.astype(BF16)
        else:
            column = jnp.concatenate(
                [jnp.sum(to_key, axis=1, keepdims=True), jnp.sum(to_val, axis=1, keepdims=True)],
                axis=0,
            )
            virt_t = jnp.where(lane == k - degree, column, virt_t)
    out_b = out_sum.astype(BF16)
    dq_b = dq_sum.astype(BF16)

    slot_grad = contract(edge_grad[...], named[...], 1, 1).astype(BF16)
    slot_feat[...] = contract(slot_grad, w_keyval[...], 0, 1).astype(BF16)
    halo_feat[...] = contract(
        kv_grad[:, 0:TILE].astype(BF16), w_keyval[...], 0, 1
    ).astype(BF16)
    own_grad = kv_grad[:, TILE:].astype(BF16)
    grad_feat[...] = contract(w_query[...], dq_b, 1, 0) + contract(
        w_keyval[...], own_grad, 1, 0
    )
    virt_hi = virt_t.astype(BF16)
    virt_lo = (virt_t - virt_hi.astype(F32)).astype(BF16)
    virt_feat[...] = (
        contract(virt_hi, w_keyval[...], 0, 1) + contract(virt_lo, w_keyval[...], 0, 1)
    )[0:8]
    sum_q = contract(dq_b, feat[...], 1, 0)
    sum_kv = (
        contract(kv_grad[...].astype(BF16), ext[...], 1, 0)
        + contract(slot_grad, slotf[...], 1, 0)
        + contract(virt_hi[:, 0:VROWS], virt[...], 1, 0)
        + contract(virt_lo[:, 0:VROWS], virt[...], 1, 0)
    )
    sum_o = contract(out_b, out_grad[...], 1, 0)
    for chunk in range(width // LANES):
        cols = slice(chunk * LANES, (chunk + 1) * LANES)
        weight_sums[chunk, 0:width] = sum_q[:, cols].astype(BF16)
        weight_sums[chunk, width : 3 * width] = sum_kv[:, cols].astype(BF16)
        weight_sums[chunk, 3 * width :] = sum_o[:, cols].astype(BF16)


def gather_kernel(
    sizes,
    slot_feat,
    halo_feat,
    sums,
    virt_feat,
    slots_back,
    halo_back,
    total,
    virt_total,
    got_c,
    sum_c,
    got_y,
    sum_y,
    got_x,
    sum_x,
    got_z,
    all_x,
    all_y,
    virt_c,
    virt_y,
    virt_x,
    virt_z,
    sems_a,
    sems_h,
    sems_c,
    sems_y,
    sems_x,
    sems_z,
    sems_gx,
    sems_gy,
    sems_gc,
    sems_v,
):
    nx, nz, ny = sizes
    n_dom, n_rows = nx * nz, 2 * ny
    dom, row = lax.axis_index("dom"), lax.axis_index("rows")
    x, z = dom // nz, lax.rem(dom, nz)
    y, core = row // 2, lax.rem(row, 2)
    mate = row + 1 - 2 * core
    chunks, height = sums.shape[0], sums.shape[1]
    half, quarter, piece = height // 2, height // 2 // ny, height // 2 // ny // nx

    def block(index, size):
        return pl.ds(pl.multiple_of(index * size, 16), size)

    barrier, arrivals = greet(n_dom, n_rows)
    virt_c[core] = virt_feat[...]
    pl.semaphore_wait(barrier, arrivals)

    def y_peer(step):
        return lax.rem(y + step, ny)

    def x_peer(step):
        return lax.rem(x + step, nx)

    def z_peer(step):
        return lax.rem(z + step, nz)

    def started(copies):
        for copy in copies:
            copy.start()
        return copies

    def waited(copies):
        for copy in copies:
            copy.wait()

    def to_core(ch):
        return [
            remote(
                sums.at[ch, block(1 - core, half)],
                got_c.at[ch],
                sems_c.at[0, ch],
                sems_c.at[1, ch],
                dom,
                mate,
            )
        ]

    def to_y(ch):
        return [
            remote(
                sum_c.at[ch, block(y_peer(s), quarter)],
                got_y.at[ch, s - 1],
                sems_y.at[0, ch, s],
                sems_y.at[1, ch, s],
                dom,
                y_peer(s) * 2 + core,
            )
            for s in range(1, ny)
        ]

    def to_x(ch):
        return [
            remote(
                sum_y.at[ch, block(x_peer(s), piece)],
                got_x.at[ch, s - 1],
                sems_x.at[0, ch, s],
                sems_x.at[1, ch, s],
                x_peer(s) * nz + z,
                row,
            )
            for s in range(1, nx)
        ]

    def to_z(ch):
        return [
            remote(
                sum_x.at[ch],
                got_z.at[ch, z],
                sems_z.at[0, ch, s],
                sems_z.at[1, ch, s],
                x * nz + z_peer(s),
                row,
            )
            for s in range(1, nz)
        ]

    def all_to_x(ch):
        return [
            remote(
                all_x.at[ch, block(x, piece)],
                all_x.at[ch, block(x, piece)],
                sems_gx.at[0, ch, s],
                sems_gx.at[1, ch, s],
                x_peer(s) * nz + z,
                row,
            )
            for s in range(1, nx)
        ]

    def all_to_y(ch):
        return [
            remote(
                all_x.at[ch],
                all_y.at[ch, block(y, quarter)],
                sems_gy.at[0, ch, s],
                sems_gy.at[1, ch, s],
                dom,
                y_peer(s) * 2 + core,
            )
            for s in range(1, ny)
        ]

    def all_to_core(ch):
        return [
            remote(
                all_y.at[ch],
                total.at[ch, block(core, half)],
                sems_gc.at[0, ch],
                sems_gc.at[1, ch],
                dom,
                mate,
            )
        ]

    def slot_copy(step):
        peer = lax.rem(dom + step, n_dom)
        return remote(
            slot_feat.at[peer],
            slots_back.at[dom],
            sems_a.at[0, step],
            sems_a.at[1, step],
            peer,
            row,
        )

    def slot_start(step, carry):
        slot_copy(step).start()
        return carry

    def slot_wait(step, carry):
        slot_copy(step).wait()
        return carry

    every = range(chunks)
    core_copies = [started(to_core(ch)) for ch in every]
    virt_core = started(
        [remote(virt_feat, virt_c.at[core], sems_v.at[0, 0], sems_v.at[1, 0], dom, mate)]
    )
    halo_copy = remote(
        halo_feat, halo_back, sems_h.at[0], sems_h.at[1], dom, lax.rem(row + n_rows - 1, n_rows)
    )
    halo_copy.start()
    lax.fori_loop(1, n_dom, slot_start, 0)
    slots_back[dom] = slot_feat[dom]

    y_copies = []
    for ch in every:
        waited(core_copies[ch])
        sum_c[ch] = (
            sums[ch, block(core, half)].astype(F32) + got_c[ch].astype(F32)
        ).astype(BF16)
        y_copies.append(started(to_y(ch)))
    waited(virt_core)
    virt_y[y] = virt_c[0] + virt_c[1]
    virt_ys = started(
        [
            remote(
                virt_y.at[y],
                virt_y.at[y],
                sems_v.at[0, s],
                sems_v.at[1, s],
                dom,
                y_peer(s) * 2 + core,
            )
            for s in range(1, ny)
        ]
    )
    x_copies = []
    for ch in every:
        waited(y_copies[ch])
        acc = sum_c[ch, block(y, quarter)].astype(F32)
        for s in range(ny - 1):
            acc = acc + got_y[ch, s].astype(F32)
        sum_y[ch] = acc.astype(BF16)
        x_copies.append(started(to_x(ch)))
    waited(virt_ys)
    total_v = virt_y[0]
    for s in range(1, ny):
        total_v = total_v + virt_y[s]
    virt_x[x] = total_v
    virt_xs = started(
        [
            remote(
                virt_x.at[x],
                virt_x.at[x],
                sems_v.at[0, ny + s],
                sems_v.at[1, ny + s],
                x_peer(s) * nz + z,
                row,
            )
            for s in range(1, nx)
        ]
    )
    z_copies = []
    for ch in every:
        waited(x_copies[ch])
        acc = sum_y[ch, block(x, piece)].astype(F32)
        for s in range(nx - 1):
            acc = acc + got_x[ch, s].astype(F32)
        sum_x[ch] = acc.astype(BF16)
        z_copies.append(started(to_z(ch)))
        got_z[ch, z] = sum_x[ch]
    waited(virt_xs)
    total_v = virt_x[0]
    for s in range(1, nx):
        total_v = total_v + virt_x[s]
    virt_z[z] = total_v
    virt_zs = started(
        [
            remote(
                virt_z.at[z],
                virt_z.at[z],
                sems_v.at[0, ny + nx + s],
                sems_v.at[1, ny + nx + s],
                x * nz + z_peer(s),
                row,
            )
            for s in range(1, nz)
        ]
    )
    gx_copies = []
    for ch in every:
        waited(z_copies[ch])
        acc = got_z[ch, 0].astype(F32)
        for s in range(1, nz):
            acc = acc + got_z[ch, s].astype(F32)
        all_x[ch, block(x, piece)] = acc.astype(BF16)
        gx_copies.append(started(all_to_x(ch)))
    waited(virt_zs)
    total_v = virt_z[0]
    for s in range(1, nz):
        total_v = total_v + virt_z[s]
    virt_total[...] = total_v
    gy_copies = []
    for ch in every:
        waited(gx_copies[ch])
        gy_copies.append(started(all_to_y(ch)))
        all_y[ch, block(y, quarter)] = all_x[ch]
    gc_copies = []
    for ch in every:
        waited(gy_copies[ch])
        gc_copies.append(started(all_to_core(ch)))
        total[ch, block(core, half)] = all_y[ch]
    for ch in every:
        waited(gc_copies[ch])
    halo_copy.wait()
    lax.fori_loop(1, n_dom, slot_wait, 0)


def finish_kernel(
    factor, send_flat, slots_back, halo_back, total, virt_total, grad_feat, gf, gq, gkv, go, gv
):
    row_count, width = gf.shape
    picker = row_picker(send_flat[...], row_count)
    summed = grad_feat[...].T + contract(picker, slots_back[...], 1, 0)
    gf[0 : row_count - TILE] = summed[0 : row_count - TILE]
    gf[row_count - TILE :] = summed[row_count - TILE :] + halo_back[...].astype(F32)
    for chunk in range(width // LANES):
        cols = slice(chunk * LANES, (chunk + 1) * LANES)
        part = total[chunk].astype(F32) * factor
        gq[cols, :] = part[0:width].T
        gkv[cols, 0:width] = part[width : 2 * width].T
        gkv[cols, width:] = part[2 * width : 3 * width].T
        go[:, cols] = part[3 * width :]
    gv[...] = virt_total[0:4] * factor


def shards(sizes, features, out_grad, w_query, w_keyval, w_out, virtual, local_nbr, expander, send_rows):
    nx, nz, ny = sizes
    n_dom, n_rows = nx * nz, 2 * ny
    rows, width = features.shape
    per_peer = send_rows.shape[1]
    slots = n_dom * per_peer
    send_flat = send_rows.reshape(1, slots)
    dma, shape = pltpu.SemaphoreType.DMA, jax.ShapeDtypeStruct
    slotf, halo = pl.pallas_call(
        functools.partial(spread_kernel, n_dom, n_rows),
        name="spread",
        out_shape=(shape((n_dom, per_peer, width), BF16), shape((TILE, width), BF16)),
        in_specs=[VMEM] * 2,
        out_specs=(VMEM, VMEM),
        scratch_shapes=[
            pltpu.VMEM((n_dom, per_peer, width), BF16),
            dma((n_dom,)),
            dma((n_dom,)),
            dma(()),
            dma(()),
        ],
        compiler_params=pltpu.CompilerParams(collective_id=0, has_side_effects=True),
    )(send_flat, features)

    slot_feat, halo_feat, sums, virt_feat, grad_feat = pl.pallas_call(
        attend_kernel,
        name="attend",
        out_shape=(
            shape((slots, width), BF16),
            shape((TILE, width), BF16),
            shape((width // LANES, 4 * width, LANES), BF16),
            shape((8, width), F32),
            shape((width, rows), F32),
        ),
        in_specs=[VMEM] * 10,
        out_specs=(VMEM,) * 5,
        scratch_shapes=[
            pltpu.VMEM((rows + TILE, width), BF16),
            pltpu.VMEM((width, rows), BF16),
            pltpu.VMEM((width, rows), BF16),
            pltpu.VMEM((2 * width, rows + TILE), BF16),
            pltpu.VMEM((2 * width, slots), BF16),
            pltpu.VMEM((slots, 4 * rows), BF16),
            pltpu.VMEM((4, 2 * width, rows), BF16),
            pltpu.VMEM((2 * TILE, rows), F32),
            pltpu.VMEM((HEADS, 8, rows), F32),
            pltpu.VMEM((HEADS, 8, rows), F32),
            pltpu.VMEM((HEADS, 8, rows), F32),
            pltpu.VMEM((HEADS, 8, rows), F32),
            pltpu.VMEM((2 * width, rows + TILE), F32),
            pltpu.VMEM((width, rows), F32),
            pltpu.VMEM((width, rows), F32),
            pltpu.VMEM((2 * width, 4 * rows), BF16),
        ],
        compiler_params=pltpu.CompilerParams(vmem_limit_bytes=60 << 20),
    )(
        features,
        halo,
        slotf.reshape(slots, width),
        out_grad,
        w_query,
        w_keyval,
        w_out,
        jnp.pad(virtual, ((0, VROWS - virtual.shape[0]), (0, 0))),
        local_nbr.T,
        expander.T,
    )

    chunks, height = sums.shape[0], sums.shape[1]
    half = height // 2
    quarter = half // ny
    piece = quarter // nx
    slots_back, halo_back, total, virt_total = pl.pallas_call(
        functools.partial(gather_kernel, sizes),
        name="gather",
        out_shape=(
            shape((n_dom, per_peer, width), BF16),
            shape((TILE, width), BF16),
            shape(sums.shape, BF16),
            shape((8, width), F32),
        ),
        in_specs=[VMEM] * 4,
        out_specs=(VMEM,) * 4,
        scratch_shapes=[
            pltpu.VMEM((chunks, half, LANES), BF16),
            pltpu.VMEM((chunks, half, LANES), BF16),
            pltpu.VMEM((chunks, ny - 1, quarter, LANES), BF16),
            pltpu.VMEM((chunks, quarter, LANES), BF16),
            pltpu.VMEM((chunks, nx - 1, piece, LANES), BF16),
            pltpu.VMEM((chunks, piece, LANES), BF16),
            pltpu.VMEM((chunks, nz, piece, LANES), BF16),
            pltpu.VMEM((chunks, quarter, LANES), BF16),
            pltpu.VMEM((chunks, half, LANES), BF16),
            pltpu.VMEM((2, 8, width), F32),
            pltpu.VMEM((ny, 8, width), F32),
            pltpu.VMEM((nx, 8, width), F32),
            pltpu.VMEM((nz, 8, width), F32),
            dma((2, n_dom)),
            dma((2,)),
            dma((2, chunks)),
            dma((2, chunks, ny)),
            dma((2, chunks, nx)),
            dma((2, chunks, nz)),
            dma((2, chunks, nx)),
            dma((2, chunks, ny)),
            dma((2, chunks)),
            dma((2, nx + ny + nz)),
        ],
        compiler_params=pltpu.CompilerParams(collective_id=1, has_side_effects=True),
    )(slot_feat.reshape(n_dom, per_peer, width), halo_feat, sums, virt_feat)

    return pl.pallas_call(
        functools.partial(finish_kernel, (rows * n_dom * n_rows) ** (-0.5)),
        name="finish",
        out_shape=(
            shape((rows, width), F32),
            shape((width, width), F32),
            shape((width, 2 * width), F32),
            shape((width, width), F32),
            shape((virtual.shape[0], width), F32),
        ),
        in_specs=[VMEM] * 6,
        out_specs=(VMEM,) * 5,
    )(send_flat, slots_back.reshape(slots, width), halo_back, total, virt_total, grad_feat)


def solution(mesh):
    n_dom, n_rows = mesh.shape["dom"], mesh.shape["rows"]
    nx = 4 if n_dom % 32 == 0 else 2
    sizes = (nx, n_dom // nx, n_rows // 2)
    across = P(("dom", "rows"), None)
    placed = (across, across, P(), P(), P(), P(), across, across, across)
    return jax.shard_map(
        functools.partial(shards, sizes),
        mesh=mesh,
        in_specs=placed,
        out_specs=(across, P(), P(), P(), P()),
        check_vma=False,
    )
```

```python
import functools
import math

import jax
import jax.numpy as jnp
from jax import lax
from jax.experimental import pallas as pl
from jax.experimental.pallas import tpu as pltpu
from jax.sharding import PartitionSpec as P

HEADS = 8
TILE = 128
LANES = 128
VROWS = 16
NEGATIVE_FILL = -1e30

F32 = jnp.float32
BF16 = jnp.bfloat16
VMEM = pl.BlockSpec(memory_space=pltpu.VMEM)


def contract(left, right, left_dim, right_dim):
    return lax.dot_general(
        left, right, (((left_dim,), (right_dim,)), ((), ())), preferred_element_type=F32
    )


def remote(src, dst, send_sem, recv_sem, dom, row):
    return pltpu.make_async_remote_copy(
        src_ref=src,
        dst_ref=dst,
        send_sem=send_sem,
        recv_sem=recv_sem,
        device_id=(dom, row),
        device_id_type=pl.DeviceIdType.MESH,
    )


def greet(n_dom, n_rows):
    dom, row = lax.axis_index("dom"), lax.axis_index("rows")
    barrier = pltpu.get_barrier_semaphore()

    def dom_peer(step, carry):
        pl.semaphore_signal(
            barrier,
            inc=1,
            device_id=(lax.rem(dom + step, n_dom), row),
            device_id_type=pl.DeviceIdType.MESH,
        )
        return carry

    def row_peer(step, carry):
        pl.semaphore_signal(
            barrier,
            inc=1,
            device_id=(dom, lax.rem(row + step, n_rows)),
            device_id_type=pl.DeviceIdType.MESH,
        )
        return carry

    lax.fori_loop(1, n_dom, dom_peer, 0)
    lax.fori_loop(1, n_rows, row_peer, 0)
    return barrier, n_dom + n_rows - 2


def whole_kernel(
    sizes,
    feat,
    out_grad,
    w_query,
    w_keyval,
    w_out,
    virt,
    local_nbr,
    expander,
    send_rows,
    grad_feat,
    total,
    virt_total,
    picker,
    picked,
    slots,
    halo,
    virt_pad,
    wkv_t,
    ext_t,
    slot_t,
    q_t,
    d_t,
    kv_t,
    named,
    bias,
    edge_kv,
    weight_e,
    weight_dp,
    rows_s,
    rows_f,
    rows_d,
    kv_grad,
    out_t,
    dq_t,
    edge_grad,
    slot_grad,
    slot_feat,
    halo_feat,
    slots_back,
    halo_back,
    sums,
    got_c,
    sum_c,
    got_y,
    sum_y,
    got_x,
    sum_x,
    got_z,
    all_x,
    all_y,
    virt_feat,
    virt_c,
    virt_y,
    virt_x,
    virt_z,
    sems_s,
    sems_g,
    sems_a,
    sems_h,
    sems_c,
    sems_y,
    sems_x,
    sems_z,
    sems_gx,
    sems_gy,
    sems_gc,
    sems_v,
):
    nx, nz, ny = sizes
    n_dom, n_rows = nx * nz, 2 * ny
    dom, row = lax.axis_index("dom"), lax.axis_index("rows")
    x, z = dom // nz, lax.rem(dom, nz)
    y, core = row // 2, lax.rem(row, 2)
    mate = row + 1 - 2 * core
    row_count, width = feat.shape
    per_peer = send_rows.shape[1]
    slot_count = n_dom * per_peer
    head_dim = width // HEADS
    degree = expander.shape[0]
    scale = 1.0 / math.sqrt(head_dim)
    tiles = row_count // TILE
    bits = per_peer.bit_length() - 1
    groups = 4
    per_group = n_dom // groups
    span = per_group * per_peer

    barrier, arrivals = greet(n_dom, n_rows)

    spot = lax.broadcasted_iota(jnp.int32, (per_peer, slot_count), 1)
    entry = lax.broadcasted_iota(jnp.int32, (per_peer, slot_count), 0)
    spread = (jnp.bitwise_and(spot, per_peer - 1) == entry).astype(F32).astype(BF16)
    listed = contract(send_rows[...].astype(F32).astype(BF16), spread, 1, 0)
    owner = lax.broadcasted_iota(jnp.int32, (n_dom, slot_count), 0)
    column = lax.broadcasted_iota(jnp.int32, (n_dom, slot_count), 1)
    mine = jnp.right_shift(column, bits) == owner
    send_flat = jnp.sum(jnp.where(mine, listed, 0.0), axis=0, keepdims=True).astype(jnp.int32)
    rows_at = lax.broadcasted_iota(jnp.int32, (row_count, slot_count), 0)
    picker[...] = (rows_at == send_flat).astype(F32).astype(BF16)
    picked[...] = contract(picker[...], feat[...], 0, 0).astype(BF16).reshape(picked.shape)

    pl.semaphore_wait(barrier, arrivals)

    halo_copy = remote(
        feat.at[pl.ds(row_count - TILE, TILE)],
        halo,
        sems_h.at[0],
        sems_h.at[1],
        dom,
        lax.rem(row + 1, n_rows),
    )
    halo_copy.start()

    def spread_copy(step):
        peer = lax.rem(dom + step, n_dom)
        return remote(
            picked.at[peer], slots.at[step], sems_s.at[0, step], sems_s.at[1, step], peer, row
        )

    def spread_start(step, carry):
        spread_copy(step).start()
        return carry

    def spread_wait(step, carry):
        spread_copy(step).wait()
        return carry

    lax.fori_loop(1, n_dom, spread_start, 0)
    slots[0] = picked[dom]

    wkv_t[...] = w_keyval[...].T
    ext_t[:, TILE:] = feat[...].T
    q_t[...] = contract(w_query[...], ext_t[:, TILE:], 0, 0).astype(BF16)
    d_t[...] = contract(w_out[...], out_grad[...], 1, 1).astype(BF16)
    kv_t[:, TILE:] = contract(wkv_t[...], ext_t[:, TILE:], 1, 0).astype(BF16)
    virt_pad[...] = jnp.zeros_like(virt_pad)
    virt_pad[0 : virt.shape[0]] = virt[...].astype(F32)
    virt_b = virt_pad[...].astype(BF16)
    virt_kv = contract(wkv_t[...], virt_b, 1, 1).astype(BF16).astype(F32)

    positions = lax.broadcasted_iota(jnp.int32, (2 * TILE, row_count), 0)
    mask = positions == local_nbr[0:1, :]
    for place in range(1, local_nbr.shape[0]):
        mask = jnp.logical_or(mask, positions == local_nbr[place : place + 1, :])
    bias[...] = jnp.where(mask, 0.0, NEGATIVE_FILL)

    source = jnp.right_shift(expander[...], bits)
    away = dom - source
    away = jnp.where(away < 0, away + n_dom, away)
    slot_of = away * per_peer + jnp.bitwise_and(expander[...], per_peer - 1)
    slot_ids = lax.broadcasted_iota(jnp.int32, (slot_count, row_count), 0)
    for k in range(degree):
        named[:, k * row_count : (k + 1) * row_count] = (
            (slot_ids == slot_of[k : k + 1, :]).astype(F32).astype(BF16)
        )

    def per_head(product):
        return product.reshape(HEADS, head_dim, row_count).sum(axis=1)

    def virtual_edge(v):
        return jnp.broadcast_to(virt_kv[:, v : v + 1], (2 * width, row_count))

    virt_s, virt_dp = [], []
    for v in range(4):
        both = virtual_edge(v)
        virt_s.append(per_head(q_t[...].astype(F32) * both[0:width]) * scale)
        virt_dp.append(per_head(d_t[...].astype(F32) * both[width:]))

    halo_copy.wait()
    ext_t[:, 0:TILE] = halo[...].T
    kv_t[:, 0:TILE] = contract(wkv_t[...], ext_t[:, 0:TILE], 1, 0).astype(BF16)

    def places(h, t):
        own = slice(h * head_dim, (h + 1) * head_dim)
        val = slice(width + h * head_dim, width + (h + 1) * head_dim)
        return own, val, slice(t * TILE, (t + 1) * TILE), slice(t * TILE, (t + 2) * TILE)

    for h in range(HEADS):
        for t in range(tiles):
            own, val, here, window = places(h, t)
            s = contract(kv_t[own, window], q_t[own, here], 0, 0) * scale + bias[:, here]
            dp = contract(kv_t[val, window], d_t[own, here], 0, 0)
            peak = jnp.max(s, axis=0, keepdims=True)
            e = jnp.exp(s - peak)
            weight_e[h, t] = e
            weight_dp[h, t] = dp
            rows_s[h : h + 1, here] = peak
            rows_f[h : h + 1, here] = jnp.sum(e, axis=0, keepdims=True)
            rows_d[h : h + 1, here] = jnp.sum(e * dp, axis=0, keepdims=True)

    for g in range(groups):
        lax.fori_loop(max(1, g * per_group), (g + 1) * per_group, spread_wait, 0)
        held = slice(g * span, (g + 1) * span)
        slot_t[:, held] = slots[g * per_group : (g + 1) * per_group].reshape(span, width).T
        slot_kv = contract(wkv_t[...], slot_t[:, held], 1, 0).astype(BF16)
        chosen = contract(slot_kv, named[held, :], 1, 0)
        if g == 0:
            edge_kv[...] = chosen
        else:
            edge_kv[...] += chosen

    q_wide = q_t[...].astype(F32)
    d_wide = d_t[...].astype(F32)
    cols = [slice(k * row_count, (k + 1) * row_count) for k in range(degree)]
    edge_s = [per_head(q_wide * edge_kv[0:width, c]) * scale for c in cols] + virt_s
    edge_dp = [per_head(d_wide * edge_kv[width:, c]) for c in cols] + virt_dp
    peak_loc = rows_s[...]
    peak = peak_loc
    for s in edge_s:
        peak = jnp.maximum(peak, s)
    shrink = jnp.exp(peak_loc - peak)
    edge_e = [jnp.exp(s - peak) for s in edge_s]
    norm = rows_f[...] * shrink
    for e in edge_e:
        norm = norm + e
    inverse = 1.0 / norm
    edge_p = [e * inverse for e in edge_e]
    share = shrink * inverse
    delta = rows_d[...] * share
    for p, dp in zip(edge_p, edge_dp):
        delta = delta + p * dp
    rows_f[...] = share
    rows_d[...] = delta
    edge_ds = [
        (p * (dp - delta) * scale).astype(BF16).astype(F32) for p, dp in zip(edge_p, edge_dp)
    ]
    edge_p = [p.astype(BF16).astype(F32) for p in edge_p]

    def widen(values):
        return jnp.broadcast_to(values[:, None, :], (HEADS, head_dim, row_count)).reshape(
            width, row_count
        )

    out_sum = jnp.zeros((width, row_count), F32)
    dq_sum = jnp.zeros((width, row_count), F32)
    for k in range(degree):
        pk, dsk = widen(edge_p[k]), widen(edge_ds[k])
        out_sum = out_sum + pk * edge_kv[width:, cols[k]]
        dq_sum = dq_sum + dsk * edge_kv[0:width, cols[k]]
        edge_grad[0:width, cols[k]] = (dsk * q_wide).astype(BF16)
        edge_grad[width:, cols[k]] = (pk * d_wide).astype(BF16)
    out_t[...] = out_sum
    dq_t[...] = dq_sum

    def back_copy(step):
        peer = lax.rem(dom - step + n_dom, n_dom)
        return remote(
            slot_feat.at[step],
            slots_back.at[dom],
            sems_g.at[0, step],
            sems_g.at[1, step],
            peer,
            row,
        )

    def back_start(step, carry):
        back_copy(step).start()
        return carry

    def back_wait(step, carry):
        back_copy(step).wait()
        return carry

    for g in range(groups):
        held = slice(g * span, (g + 1) * span)
        grad_g = contract(edge_grad[...], named[held, :], 1, 1).astype(BF16)
        slot_grad[:, held] = grad_g
        slot_feat[g * per_group : (g + 1) * per_group] = (
            contract(grad_g, w_keyval[...], 0, 1).astype(BF16).reshape(per_group, per_peer, width)
        )
        lax.fori_loop(max(1, g * per_group), (g + 1) * per_group, back_start, 0)
    slots_back[dom] = slot_feat[0]

    kv_grad[...] = jnp.zeros_like(kv_grad)
    for h in range(HEADS):
        for t in range(tiles):
            own, val, here, window = places(h, t)
            p = weight_e[h, t] * rows_f[h : h + 1, here]
            ds = (p * (weight_dp[h, t] - rows_d[h : h + 1, here]) * scale).astype(BF16)
            pb = p.astype(BF16)
            out_t[own, here] += contract(kv_t[val, window], pb, 1, 0)
            dq_t[own, here] += contract(kv_t[own, window], ds, 1, 0)
            kv_grad[own, window] += contract(q_t[own, here], ds, 1, 1)
            kv_grad[val, window] += contract(d_t[own, here], pb, 1, 1)

    lane = lax.broadcasted_iota(jnp.int32, (2 * width, LANES), 1)
    virt_t = jnp.zeros((2 * width, LANES), F32)
    out_sum = out_t[...]
    dq_sum = dq_t[...]
    for v in range(4):
        pk, dsk = widen(edge_p[degree + v]), widen(edge_ds[degree + v])
        both = virtual_edge(v)
        out_sum = out_sum + pk * both[width:]
        dq_sum = dq_sum + dsk * both[0:width]
        to_both = jnp.concatenate(
            [
                jnp.sum(dsk * q_wide, axis=1, keepdims=True),
                jnp.sum(pk * d_wide, axis=1, keepdims=True),
            ],
            axis=0,
        )
        virt_t = jnp.where(lane == v, to_both, virt_t)
    out_b = out_sum.astype(BF16)
    dq_b = dq_sum.astype(BF16)

    chunks, height = sums.shape[0], sums.shape[1]
    half, quarter, piece = height // 2, height // 2 // ny, height // 2 // ny // nx

    def put(block_index, value):
        first = block_index * width
        while value.shape[0]:
            ch, at = divmod(first, height)
            count = min(height - at, value.shape[0])
            sums[ch, at : at + count] = value[0:count]
            value = value[count:]
            first += count

    def block(index, size):
        return pl.ds(pl.multiple_of(index * size, 16), size)

    def y_peer(step):
        return lax.rem(y + step, ny)

    def x_peer(step):
        return lax.rem(x + step, nx)

    def z_peer(step):
        return lax.rem(z + step, nz)

    started = {}

    def start(key, copies):
        for copy in copies:
            copy.start()
        started[key] = copies

    def finish(key):
        for copy in started.pop(key):
            copy.wait()

    def stage_c(ch):
        start(
            ("c", ch),
            [
                remote(
                    sums.at[ch, block(1 - core, half)],
                    got_c.at[ch],
                    sems_c.at[0, ch],
                    sems_c.at[1, ch],
                    dom,
                    mate,
                )
            ],
        )

    def stage_y(ch):
        finish(("c", ch))
        sum_c[ch] = (sums[ch, block(core, half)].astype(F32) + got_c[ch].astype(F32)).astype(BF16)
        start(
            ("y", ch),
            [
                remote(
                    sum_c.at[ch, block(y_peer(s), quarter)],
                    got_y.at[ch, s - 1],
                    sems_y.at[0, ch, s],
                    sems_y.at[1, ch, s],
                    dom,
                    y_peer(s) * 2 + core,
                )
                for s in range(1, ny)
            ],
        )

    def stage_x(ch):
        finish(("y", ch))
        acc = sum_c[ch, block(y, quarter)].astype(F32)
        for s in range(ny - 1):
            acc = acc + got_y[ch, s].astype(F32)
        sum_y[ch] = acc.astype(BF16)
        start(
            ("x", ch),
            [
                remote(
                    sum_y.at[ch, block(x_peer(s), piece)],
                    got_x.at[ch, s - 1],
                    sems_x.at[0, ch, s],
                    sems_x.at[1, ch, s],
                    x_peer(s) * nz + z,
                    row,
                )
                for s in range(1, nx)
            ],
        )

    def stage_z(ch):
        finish(("x", ch))
        acc = sum_y[ch, block(x, piece)].astype(F32)
        for s in range(nx - 1):
            acc = acc + got_x[ch, s].astype(F32)
        sum_x[ch] = acc.astype(BF16)
        start(
            ("z", ch),
            [
                remote(
                    sum_x.at[ch],
                    got_z.at[ch, z],
                    sems_z.at[0, ch, s],
                    sems_z.at[1, ch, s],
                    x * nz + z_peer(s),
                    row,
                )
                for s in range(1, nz)
            ],
        )
        got_z[ch, z] = acc.astype(BF16)

    def stage_all_x(ch):
        finish(("z", ch))
        acc = got_z[ch, 0].astype(F32)
        for s in range(1, nz):
            acc = acc + got_z[ch, s].astype(F32)
        all_x[ch, block(x, piece)] = acc.astype(BF16)
        start(
            ("gx", ch),
            [
                remote(
                    all_x.at[ch, block(x, piece)],
                    all_x.at[ch, block(x, piece)],
                    sems_gx.at[0, ch, s],
                    sems_gx.at[1, ch, s],
                    x_peer(s) * nz + z,
                    row,
                )
                for s in range(1, nx)
            ],
        )

    def stage_all_y(ch):
        finish(("gx", ch))
        start(
            ("gy", ch),
            [
                remote(
                    all_x.at[ch],
                    all_y.at[ch, block(y, quarter)],
                    sems_gy.at[0, ch, s],
                    sems_gy.at[1, ch, s],
                    dom,
                    y_peer(s) * 2 + core,
                )
                for s in range(1, ny)
            ],
        )
        all_y[ch, block(y, quarter)] = all_x[ch]

    def stage_all_c(ch):
        finish(("gy", ch))
        start(
            ("gc", ch),
            [
                remote(
                    all_y.at[ch],
                    total.at[ch, block(core, half)],
                    sems_gc.at[0, ch],
                    sems_gc.at[1, ch],
                    dom,
                    mate,
                )
            ],
        )
        total[ch, block(core, half)] = all_y[ch]

    def virt_exchange(key, buffer, index, first, peers):
        start(
            key,
            [
                remote(
                    buffer.at[index],
                    buffer.at[index],
                    sems_v.at[0, first + s],
                    sems_v.at[1, first + s],
                    to_dom,
                    to_row,
                )
                for s, (to_dom, to_row) in enumerate(peers)
            ],
        )

    def virt_sum(key, buffer):
        finish(key)
        acc = buffer[0]
        for s in range(1, buffer.shape[0]):
            acc = acc + buffer[s]
        return acc

    def virt_stage(stage):
        if stage == 0:
            virt_c[core] = virt_feat[...]
            virt_exchange("vc", virt_c, core, 0, [(dom, mate)])
        elif stage == 1:
            virt_y[y] = virt_sum("vc", virt_c)
            virt_exchange(
                "vy", virt_y, y, 1, [(dom, y_peer(s) * 2 + core) for s in range(1, ny)]
            )
        elif stage == 2:
            virt_x[x] = virt_sum("vy", virt_y)
            virt_exchange(
                "vx", virt_x, x, ny, [(x_peer(s) * nz + z, row) for s in range(1, nx)]
            )
        elif stage == 3:
            virt_z[z] = virt_sum("vx", virt_x)
            virt_exchange(
                "vz", virt_z, z, ny + nx - 1, [(x * nz + z_peer(s), row) for s in range(1, nz)]
            )
        elif stage == 4:
            virt_total[...] = virt_sum("vz", virt_z)

    stages = [stage_c, stage_y, stage_x, stage_z, stage_all_x, stage_all_y, stage_all_c]

    put(0, contract(out_b, out_grad[...], 1, 0).astype(BF16))
    put(1, contract(ext_t[:, TILE:], dq_b, 1, 1).astype(BF16))
    stage_c(0)
    virt_hi = virt_t.astype(BF16)
    virt_lo = (virt_t - virt_hi.astype(F32)).astype(BF16)
    kv_sum = (
        contract(ext_t[...], kv_grad[...].astype(BF16), 1, 1)
        + contract(slot_t[...], slot_grad[...], 1, 1)
        + contract(virt_b, virt_hi[:, 0:VROWS], 0, 1)
        + contract(virt_b, virt_lo[:, 0:VROWS], 0, 1)
    ).astype(BF16)
    put(2, kv_sum[:, 0:width])
    put(3, kv_sum[:, width:])
    stage_c(1)
    stage_c(2)
    virt_feat[...] = (
        contract(virt_hi, w_keyval[...], 0, 1) + contract(virt_lo, w_keyval[...], 0, 1)
    )[0:8]
    virt_stage(0)
    halo_feat[...] = contract(kv_grad[:, 0:TILE].astype(BF16), w_keyval[...], 0, 1).astype(BF16)
    halo_return = remote(
        halo_feat,
        halo_back,
        sems_a.at[0],
        sems_a.at[1],
        dom,
        lax.rem(row + n_rows - 1, n_rows),
    )
    halo_return.start()
    stage_y(0)
    stage_y(1)
    stage_y(2)
    grad_t = contract(w_query[...], dq_b, 1, 0) + contract(
        w_keyval[...], kv_grad[:, TILE:].astype(BF16), 1, 0
    )
    grad_feat[...] = grad_t.T
    for diagonal in range(2, len(stages) + chunks):
        for ch in range(chunks):
            stage = diagonal - ch
            if 2 <= stage < len(stages):
                stages[stage](ch)
        virt_stage(diagonal - 1)
    halo_return.wait()
    lax.fori_loop(1, n_dom, back_wait, 0)
    summed = grad_feat[...] + contract(
        picker[...], slots_back[...].reshape(slot_count, width), 1, 0
    )
    grad_feat[0 : row_count - TILE] = summed[0 : row_count - TILE]
    grad_feat[row_count - TILE :] = summed[row_count - TILE :] + halo_back[...].astype(F32)
    for ch in range(chunks):
        finish(("gc", ch))


def finish_kernel(factor, go_in, gq_in, gk_in, gv_in, virt_in, feat_in, gq, gkv, go, gv, gf):
    width = gq.shape[1]
    gq[...] = gq_in[...].astype(F32) * factor
    go[...] = go_in[...].astype(F32) * factor
    gkv[:, 0:width] = gk_in[...].astype(F32) * factor
    gkv[:, width:] = gv_in[...].astype(F32) * factor

    @pl.when(pl.program_id(0) == 0)
    def _():
        gv[...] = virt_in[0 : gv.shape[0]] * factor
        gf[...] = feat_in[...]


def shards(sizes, features, out_grad, w_query, w_keyval, w_out, virtual, local_nbr, expander, send_rows):
    nx, nz, ny = sizes
    n_dom, n_rows = nx * nz, 2 * ny
    rows, width = features.shape
    per_peer = send_rows.shape[1]
    slots = n_dom * per_peer
    dma, shape = pltpu.SemaphoreType.DMA, jax.ShapeDtypeStruct
    chunks = 3
    height = 4 * width // chunks
    half = height // 2
    quarter = half // ny
    piece = quarter // nx
    tiles = rows // TILE
    grad_feat, total, virt_total = pl.pallas_call(
        functools.partial(whole_kernel, sizes),
        name="whole",
        out_shape=(
            shape((rows, width), F32),
            shape((chunks, height, width), BF16),
            shape((8, width), F32),
        ),
        in_specs=[VMEM] * 9,
        out_specs=(VMEM,) * 3,
        scratch_shapes=[
            pltpu.VMEM((rows, slots), BF16),
            pltpu.VMEM((n_dom, per_peer, width), BF16),
            pltpu.VMEM((n_dom, per_peer, width), BF16),
            pltpu.VMEM((TILE, width), BF16),
            pltpu.VMEM((VROWS, width), F32),
            pltpu.VMEM((2 * width, width), BF16),
            pltpu.VMEM((width, rows + TILE), BF16),
            pltpu.VMEM((width, slots), BF16),
            pltpu.VMEM((width, rows), BF16),
            pltpu.VMEM((width, rows), BF16),
            pltpu.VMEM((2 * width, rows + TILE), BF16),
            pltpu.VMEM((slots, 4 * rows), BF16),
            pltpu.VMEM((2 * TILE, rows), F32),
            pltpu.VMEM((2 * width, 4 * rows), F32),
            pltpu.VMEM((HEADS, tiles, 2 * TILE, TILE), F32),
            pltpu.VMEM((HEADS, tiles, 2 * TILE, TILE), F32),
            pltpu.VMEM((HEADS, rows), F32),
            pltpu.VMEM((HEADS, rows), F32),
            pltpu.VMEM((HEADS, rows), F32),
            pltpu.VMEM((2 * width, rows + TILE), F32),
            pltpu.VMEM((width, rows), F32),
            pltpu.VMEM((width, rows), F32),
            pltpu.VMEM((2 * width, 4 * rows), BF16),
            pltpu.VMEM((2 * width, slots), BF16),
            pltpu.VMEM((n_dom, per_peer, width), BF16),
            pltpu.VMEM((TILE, width), BF16),
            pltpu.VMEM((n_dom, per_peer, width), BF16),
            pltpu.VMEM((TILE, width), BF16),
            pltpu.VMEM((chunks, height, width), BF16),
            pltpu.VMEM((chunks, half, width), BF16),
            pltpu.VMEM((chunks, half, width), BF16),
            pltpu.VMEM((chunks, ny - 1, quarter, width), BF16),
            pltpu.VMEM((chunks, quarter, width), BF16),
            pltpu.VMEM((chunks, nx - 1, piece, width), BF16),
            pltpu.VMEM((chunks, piece, width), BF16),
            pltpu.VMEM((chunks, nz, piece, width), BF16),
            pltpu.VMEM((chunks, quarter, width), BF16),
            pltpu.VMEM((chunks, half, width), BF16),
            pltpu.VMEM((8, width), F32),
            pltpu.VMEM((2, 8, width), F32),
            pltpu.VMEM((ny, 8, width), F32),
            pltpu.VMEM((nx, 8, width), F32),
            pltpu.VMEM((nz, 8, width), F32),
            dma((2, n_dom)),
            dma((2, n_dom)),
            dma((2,)),
            dma((2,)),
            dma((2, chunks)),
            dma((2, chunks, ny)),
            dma((2, chunks, nx)),
            dma((2, chunks, nz)),
            dma((2, chunks, nx)),
            dma((2, chunks, ny)),
            dma((2, chunks)),
            dma((2, nx + ny + nz)),
        ],
        compiler_params=pltpu.CompilerParams(
            collective_id=0, has_side_effects=True, vmem_limit_bytes=60 << 20
        ),
    )(
        features,
        out_grad,
        w_query,
        w_keyval,
        w_out,
        virtual,
        local_nbr.T,
        expander.T,
        send_rows,
    )

    flat = total.reshape(chunks * height, width)
    steps = width // LANES

    def rows_of(part):
        return pl.BlockSpec((LANES, width), lambda i: (part * steps + i, 0))

    def fixed(count):
        return pl.BlockSpec((count, width), lambda i: (0, 0))

    gq, gkv, go, gv, gf = pl.pallas_call(
        functools.partial(finish_kernel, (rows * n_dom * n_rows) ** (-0.5)),
        name="finish",
        grid=(steps,),
        out_shape=(
            shape((width, width), F32),
            shape((width, 2 * width), F32),
            shape((width, width), F32),
            shape((virtual.shape[0], width), F32),
            shape((rows, width), F32),
        ),
        in_specs=[rows_of(0), rows_of(1), rows_of(2), rows_of(3), fixed(8), fixed(rows)],
        out_specs=(
            rows_of(0),
            pl.BlockSpec((LANES, 2 * width), lambda i: (i, 0)),
            rows_of(0),
            fixed(virtual.shape[0]),
            fixed(rows),
        ),
    )(flat, flat, flat, flat, virt_total, grad_feat)
    return gf, gq, gkv, go, gv


def solution(mesh):
    n_dom, n_rows = mesh.shape["dom"], mesh.shape["rows"]
    nx = 4 if n_dom % 32 == 0 else 2
    sizes = (nx, n_dom // nx, n_rows // 2)
    across = P(("dom", "rows"), None)
    placed = (across, across, P(), P(), P(), P(), across, across, across)
    return jax.shard_map(
        functools.partial(shards, sizes),
        mesh=mesh,
        in_specs=placed,
        out_specs=(across, P(), P(), P(), P()),
        check_vma=False,
    )
```

```python
import functools
import heapq
import math

import jax
import jax.numpy as jnp
from jax import lax
from jax.experimental import pallas as pl
from jax.experimental.pallas import tpu as pltpu
from jax.sharding import PartitionSpec as P

HEADS = 8
TILE = 128
LANES = 128
VROWS = 16
NEGATIVE_FILL = -1e30

F32 = jnp.float32
BF16 = jnp.bfloat16
VMEM = pl.BlockSpec(memory_space=pltpu.VMEM)


def contract(left, right, left_dim, right_dim):
    return lax.dot_general(
        left, right, (((left_dim,), (right_dim,)), ((), ())), preferred_element_type=F32
    )


def remote(src, dst, send_sem, recv_sem, dom, row):
    return pltpu.make_async_remote_copy(
        src_ref=src,
        dst_ref=dst,
        send_sem=send_sem,
        recv_sem=recv_sem,
        device_id=(dom, row),
        device_id_type=pl.DeviceIdType.MESH,
    )


def greet(n_dom, n_rows):
    dom, row = lax.axis_index("dom"), lax.axis_index("rows")
    barrier = pltpu.get_barrier_semaphore()

    def dom_peer(step, carry):
        pl.semaphore_signal(
            barrier,
            inc=1,
            device_id=(lax.rem(dom + step, n_dom), row),
            device_id_type=pl.DeviceIdType.MESH,
        )
        return carry

    def row_peer(step, carry):
        pl.semaphore_signal(
            barrier,
            inc=1,
            device_id=(dom, lax.rem(row + step, n_rows)),
            device_id_type=pl.DeviceIdType.MESH,
        )
        return carry

    lax.fori_loop(1, n_dom, dom_peer, 0)
    lax.fori_loop(1, n_rows, row_peer, 0)
    return barrier, n_dom + n_rows - 2


def wave_order(first):
    chunks = len(first)
    track = ["c", "y", "x", "z", "x", "y", "c"]
    load = [1.5, 6.5, 2.0, 6.5, 2.0, 6.5, 1.5]
    lag = [0.8, 1.8, 1.8, 3.5, 1.8, 1.8, 0.8]
    free = {name: 0.0 for name in track}
    ready = [(start, ch, 0) for ch, start in enumerate(first)]
    heapq.heapify(ready)
    order = []
    while ready:
        now, ch, stage = heapq.heappop(ready)
        order.append((stage, ch))
        if stage + 1 < len(track):
            begin = max(now, free[track[stage]])
            free[track[stage]] = begin + load[stage] / chunks
            heapq.heappush(ready, (free[track[stage]] + lag[stage], ch, stage + 1))
    return order


def whole_kernel(
    sizes,
    feat_in,
    out_grad_in,
    w_query_in,
    w_keyval_in,
    w_out_in,
    virt,
    local_nbr,
    expander,
    send_rows,
    grad_feat,
    total,
    virt_total,
    feat,
    out_grad,
    w_query,
    w_keyval,
    w_out,
    picker,
    picked,
    slots,
    halo,
    virt_pad,
    wkv_t,
    ext_t,
    edge_x,
    edge_x_sum,
    q_t,
    d_t,
    kv_t,
    named,
    bias,
    edge_kv,
    weight_e,
    weight_dp,
    rows_s,
    rows_f,
    rows_d,
    kv_grad,
    out_t,
    dq_t,
    edge_grad,
    edge_feat,
    slot_feat,
    halo_feat,
    slots_back,
    halo_back,
    sums,
    got_c,
    sum_c,
    got_y,
    sum_y,
    got_x,
    sum_x,
    got_z,
    all_x,
    all_y,
    virt_feat,
    virt_c,
    virt_y,
    virt_x,
    virt_z,
    sems_in,
    sems_s,
    sems_g,
    sems_a,
    sems_h,
    sems_c,
    sems_y,
    sems_x,
    sems_z,
    sems_gx,
    sems_gy,
    sems_gc,
    sems_v,
):
    nx, nz, ny = sizes
    n_dom, n_rows = nx * nz, 2 * ny
    dom, row = lax.axis_index("dom"), lax.axis_index("rows")
    x, z = dom // nz, lax.rem(dom, nz)
    y, core = row // 2, lax.rem(row, 2)
    mate = row + 1 - 2 * core
    row_count, width = feat.shape
    per_peer = send_rows.shape[1]
    slot_count = n_dom * per_peer
    head_dim = width // HEADS
    degree = expander.shape[0]
    scale = 1.0 / math.sqrt(head_dim)
    tiles = row_count // TILE
    bits = per_peer.bit_length() - 1
    groups = 4
    per_group = n_dom // groups
    span = per_group * per_peer

    barrier, arrivals = greet(n_dom, n_rows)
    loads = [
        pltpu.make_async_copy(src, dst, sems_in.at[i])
        for i, (src, dst) in enumerate(
            [
                (feat_in, feat),
                (w_keyval_in, w_keyval),
                (w_query_in, w_query),
                (w_out_in, w_out),
                (out_grad_in, out_grad),
            ]
        )
    ]
    for load in loads:
        load.start()

    spot = lax.broadcasted_iota(jnp.int32, (per_peer, slot_count), 1)
    entry = lax.broadcasted_iota(jnp.int32, (per_peer, slot_count), 0)
    spread = (jnp.bitwise_and(spot, per_peer - 1) == entry).astype(F32).astype(BF16)
    listed = contract(send_rows[...].astype(F32).astype(BF16), spread, 1, 0)
    owner = lax.broadcasted_iota(jnp.int32, (n_dom, slot_count), 0)
    column = lax.broadcasted_iota(jnp.int32, (n_dom, slot_count), 1)
    mine = jnp.right_shift(column, bits) == owner
    send_flat = jnp.sum(jnp.where(mine, listed, 0.0), axis=0, keepdims=True).astype(jnp.int32)
    rows_at = lax.broadcasted_iota(jnp.int32, (row_count, slot_count), 0)
    picker[...] = (rows_at == send_flat).astype(F32).astype(BF16)
    loads[0].wait()
    picked[...] = contract(picker[...], feat[...], 0, 0).astype(BF16).reshape(picked.shape)

    pl.semaphore_wait(barrier, arrivals)

    halo_copy = remote(
        feat.at[pl.ds(row_count - TILE, TILE)],
        halo,
        sems_h.at[0],
        sems_h.at[1],
        dom,
        lax.rem(row + 1, n_rows),
    )
    halo_copy.start()

    def spread_copy(step):
        peer = lax.rem(dom + step, n_dom)
        return remote(
            picked.at[peer], slots.at[step], sems_s.at[0, step], sems_s.at[1, step], peer, row
        )

    def spread_start(step, carry):
        spread_copy(step).start()
        return carry

    def spread_wait(step, carry):
        spread_copy(step).wait()
        return carry

    lax.fori_loop(1, n_dom, spread_start, 0)
    slots[0] = picked[dom]

    for load in loads[1:]:
        load.wait()
    wkv_t[...] = w_keyval[...].T
    ext_t[:, TILE:] = feat[...].T
    q_t[...] = contract(w_query[...], ext_t[:, TILE:], 0, 0).astype(BF16)
    d_t[...] = contract(w_out[...], out_grad[...], 1, 1).astype(BF16)
    kv_t[:, TILE:] = contract(wkv_t[...], ext_t[:, TILE:], 1, 0).astype(BF16)
    virt_pad[...] = jnp.zeros_like(virt_pad)
    virt_pad[0 : virt.shape[0]] = virt[...].astype(F32)
    virt_b = virt_pad[...].astype(BF16)
    virt_kv = contract(wkv_t[...], virt_b, 1, 1).astype(BF16).astype(F32)

    positions = lax.broadcasted_iota(jnp.int32, (2 * TILE, row_count), 0)
    mask = positions == local_nbr[0:1, :]
    for place in range(1, local_nbr.shape[0]):
        mask = jnp.logical_or(mask, positions == local_nbr[place : place + 1, :])
    bias[...] = jnp.where(mask, 0.0, NEGATIVE_FILL)

    source = jnp.right_shift(expander[...], bits)
    away = dom - source
    away = jnp.where(away < 0, away + n_dom, away)
    slot_of = away * per_peer + jnp.bitwise_and(expander[...], per_peer - 1)
    slot_ids = lax.broadcasted_iota(jnp.int32, (slot_count, row_count), 0)
    for k in range(degree):
        named[:, k * row_count : (k + 1) * row_count] = (
            (slot_ids == slot_of[k : k + 1, :]).astype(F32).astype(BF16)
        )

    def per_head(product):
        return product.reshape(HEADS, head_dim, row_count).sum(axis=1)

    def virtual_edge(v):
        return jnp.broadcast_to(virt_kv[:, v : v + 1], (2 * width, row_count))

    virt_s, virt_dp = [], []
    for v in range(4):
        both = virtual_edge(v)
        virt_s.append(per_head(q_t[...].astype(F32) * both[0:width]) * scale)
        virt_dp.append(per_head(d_t[...].astype(F32) * both[width:]))

    halo_copy.wait()
    ext_t[:, 0:TILE] = halo[...].T
    kv_t[:, 0:TILE] = contract(wkv_t[...], ext_t[:, 0:TILE], 1, 0).astype(BF16)

    def places(h, t):
        own = slice(h * head_dim, (h + 1) * head_dim)
        val = slice(width + h * head_dim, width + (h + 1) * head_dim)
        return own, val, slice(t * TILE, (t + 1) * TILE), slice(t * TILE, (t + 2) * TILE)

    for h in range(HEADS):
        for t in range(tiles):
            own, val, here, window = places(h, t)
            s = contract(kv_t[own, window], q_t[own, here], 0, 0) * scale + bias[:, here]
            dp = contract(kv_t[val, window], d_t[own, here], 0, 0)
            peak = jnp.max(s, axis=0, keepdims=True)
            e = jnp.exp(s - peak)
            weight_e[h, t] = e
            weight_dp[h, t] = dp
            rows_s[h : h + 1, here] = peak
            rows_f[h : h + 1, here] = jnp.sum(e, axis=0, keepdims=True)
            rows_d[h : h + 1, here] = jnp.sum(e * dp, axis=0, keepdims=True)

    for g in range(groups):
        lax.fori_loop(max(1, g * per_group), (g + 1) * per_group, spread_wait, 0)
        held = slice(g * span, (g + 1) * span)
        found = contract(
            slots[g * per_group : (g + 1) * per_group].reshape(span, width), named[held, :], 0, 0
        )
        if g == 0:
            edge_x_sum[...] = found
        elif g + 1 < groups:
            edge_x_sum[...] += found
        else:
            edge_x[...] = (edge_x_sum[...] + found).astype(BF16)
    edge_kv[...] = contract(wkv_t[...], edge_x[...], 1, 0).astype(BF16).astype(F32)

    q_wide = q_t[...].astype(F32)
    d_wide = d_t[...].astype(F32)
    cols = [slice(k * row_count, (k + 1) * row_count) for k in range(degree)]
    edge_s = [per_head(q_wide * edge_kv[0:width, c]) * scale for c in cols] + virt_s
    edge_dp = [per_head(d_wide * edge_kv[width:, c]) for c in cols] + virt_dp
    peak_loc = rows_s[...]
    peak = peak_loc
    for s in edge_s:
        peak = jnp.maximum(peak, s)
    shrink = jnp.exp(peak_loc - peak)
    edge_e = [jnp.exp(s - peak) for s in edge_s]
    norm = rows_f[...] * shrink
    for e in edge_e:
        norm = norm + e
    inverse = 1.0 / norm
    edge_p = [e * inverse for e in edge_e]
    share = shrink * inverse
    delta = rows_d[...] * share
    for p, dp in zip(edge_p, edge_dp):
        delta = delta + p * dp
    rows_f[...] = share
    rows_d[...] = delta
    edge_ds = [
        (p * (dp - delta) * scale).astype(BF16).astype(F32) for p, dp in zip(edge_p, edge_dp)
    ]
    edge_p = [p.astype(BF16).astype(F32) for p in edge_p]

    def widen(values):
        return jnp.broadcast_to(values[:, None, :], (HEADS, head_dim, row_count)).reshape(
            width, row_count
        )

    out_sum = jnp.zeros((width, row_count), F32)
    dq_sum = jnp.zeros((width, row_count), F32)
    for k in range(degree):
        pk, dsk = widen(edge_p[k]), widen(edge_ds[k])
        out_sum = out_sum + pk * edge_kv[width:, cols[k]]
        dq_sum = dq_sum + dsk * edge_kv[0:width, cols[k]]
        edge_grad[0:width, cols[k]] = (dsk * q_wide).astype(BF16)
        edge_grad[width:, cols[k]] = (pk * d_wide).astype(BF16)
    out_t[...] = out_sum
    dq_t[...] = dq_sum

    def back_copy(step):
        peer = lax.rem(dom - step + n_dom, n_dom)
        return remote(
            slot_feat.at[step],
            slots_back.at[dom],
            sems_g.at[0, step],
            sems_g.at[1, step],
            peer,
            row,
        )

    def back_start(step, carry):
        back_copy(step).start()
        return carry

    def back_wait(step, carry):
        back_copy(step).wait()
        return carry

    def slot_sums(g):
        held = slice(g * span, (g + 1) * span)
        slot_feat[g * per_group : (g + 1) * per_group] = (
            contract(named[held, :], edge_feat[...], 1, 1)
            .astype(BF16)
            .reshape(per_group, per_peer, width)
        )

    def slot_return(g):
        lax.fori_loop(max(1, g * per_group), (g + 1) * per_group, back_start, 0)

    kv_grad[...] = jnp.zeros_like(kv_grad)
    for h in range(HEADS):
        for t in range(tiles):
            own, val, here, window = places(h, t)
            p = weight_e[h, t] * rows_f[h : h + 1, here]
            ds = (p * (weight_dp[h, t] - rows_d[h : h + 1, here]) * scale).astype(BF16)
            pb = p.astype(BF16)
            out_t[own, here] += contract(kv_t[val, window], pb, 1, 0)
            dq_t[own, here] += contract(kv_t[own, window], ds, 1, 0)
            kv_grad[own, window] += contract(q_t[own, here], ds, 1, 1)
            kv_grad[val, window] += contract(d_t[own, here], pb, 1, 1)

    lane = lax.broadcasted_iota(jnp.int32, (2 * width, LANES), 1)
    virt_t = jnp.zeros((2 * width, LANES), F32)
    out_sum = out_t[...]
    dq_sum = dq_t[...]
    for v in range(4):
        pk, dsk = widen(edge_p[degree + v]), widen(edge_ds[degree + v])
        both = virtual_edge(v)
        out_sum = out_sum + pk * both[width:]
        dq_sum = dq_sum + dsk * both[0:width]
        to_both = jnp.concatenate(
            [
                jnp.sum(dsk * q_wide, axis=1, keepdims=True),
                jnp.sum(pk * d_wide, axis=1, keepdims=True),
            ],
            axis=0,
        )
        virt_t = jnp.where(lane == v, to_both, virt_t)
    out_b = out_sum.astype(BF16)
    dq_b = dq_sum.astype(BF16)

    chunks, height = sums.shape[0], sums.shape[1]
    half, quarter, piece = height // 2, height // 2 // ny, height // 2 // ny // nx

    def put(block_index, value):
        first = block_index * width
        while value.shape[0]:
            ch, at = divmod(first, height)
            count = min(height - at, value.shape[0])
            sums[ch, at : at + count] = value[0:count]
            value = value[count:]
            first += count

    def block(index, size):
        return pl.ds(pl.multiple_of(index * size, 16), size)

    def y_peer(step):
        return lax.rem(y + step, ny)

    def x_peer(step):
        return lax.rem(x + step, nx)

    def z_peer(step):
        return lax.rem(z + step, nz)

    started = {}

    def start(key, copies):
        for copy in copies:
            copy.start()
        started[key] = copies

    def finish(key):
        for copy in started.pop(key):
            copy.wait()

    def stage_c(ch):
        start(
            ("c", ch),
            [
                remote(
                    sums.at[ch, block(1 - core, half)],
                    got_c.at[ch],
                    sems_c.at[0, ch],
                    sems_c.at[1, ch],
                    dom,
                    mate,
                )
            ],
        )

    def stage_y(ch):
        finish(("c", ch))
        sum_c[ch] = (sums[ch, block(core, half)].astype(F32) + got_c[ch].astype(F32)).astype(BF16)
        start(
            ("y", ch),
            [
                remote(
                    sum_c.at[ch, block(y_peer(s), quarter)],
                    got_y.at[ch, s - 1],
                    sems_y.at[0, ch, s],
                    sems_y.at[1, ch, s],
                    dom,
                    y_peer(s) * 2 + core,
                )
                for s in range(1, ny)
            ],
        )

    def stage_x(ch):
        finish(("y", ch))
        acc = sum_c[ch, block(y, quarter)].astype(F32)
        for s in range(ny - 1):
            acc = acc + got_y[ch, s].astype(F32)
        sum_y[ch] = acc.astype(BF16)
        start(
            ("x", ch),
            [
                remote(
                    sum_y.at[ch, block(x_peer(s), piece)],
                    got_x.at[ch, s - 1],
                    sems_x.at[0, ch, s],
                    sems_x.at[1, ch, s],
                    x_peer(s) * nz + z,
                    row,
                )
                for s in range(1, nx)
            ],
        )

    def stage_z(ch):
        finish(("x", ch))
        acc = sum_y[ch, block(x, piece)].astype(F32)
        for s in range(nx - 1):
            acc = acc + got_x[ch, s].astype(F32)
        sum_x[ch] = acc.astype(BF16)
        start(
            ("z", ch),
            [
                remote(
                    sum_x.at[ch],
                    got_z.at[ch, z],
                    sems_z.at[0, ch, s],
                    sems_z.at[1, ch, s],
                    x * nz + z_peer(s),
                    row,
                )
                for s in range(1, nz)
            ],
        )
        got_z[ch, z] = acc.astype(BF16)

    def stage_all_x(ch):
        finish(("z", ch))
        acc = got_z[ch, 0].astype(F32)
        for s in range(1, nz):
            acc = acc + got_z[ch, s].astype(F32)
        all_x[ch, block(x, piece)] = acc.astype(BF16)
        start(
            ("gx", ch),
            [
                remote(
                    all_x.at[ch, block(x, piece)],
                    all_x.at[ch, block(x, piece)],
                    sems_gx.at[0, ch, s],
                    sems_gx.at[1, ch, s],
                    x_peer(s) * nz + z,
                    row,
                )
                for s in range(1, nx)
            ],
        )

    def stage_all_y(ch):
        finish(("gx", ch))
        start(
            ("gy", ch),
            [
                remote(
                    all_x.at[ch],
                    all_y.at[ch, block(y, quarter)],
                    sems_gy.at[0, ch, s],
                    sems_gy.at[1, ch, s],
                    dom,
                    y_peer(s) * 2 + core,
                )
                for s in range(1, ny)
            ],
        )
        all_y[ch, block(y, quarter)] = all_x[ch]

    def stage_all_c(ch):
        finish(("gy", ch))
        start(
            ("gc", ch),
            [
                remote(
                    all_y.at[ch],
                    total.at[ch, block(core, half)],
                    sems_gc.at[0, ch],
                    sems_gc.at[1, ch],
                    dom,
                    mate,
                )
            ],
        )
        total[ch, block(core, half)] = all_y[ch]

    def virt_exchange(key, buffer, index, first, peers):
        start(
            key,
            [
                remote(
                    buffer.at[index],
                    buffer.at[index],
                    sems_v.at[0, first + s],
                    sems_v.at[1, first + s],
                    to_dom,
                    to_row,
                )
                for s, (to_dom, to_row) in enumerate(peers)
            ],
        )

    def virt_sum(key, buffer):
        finish(key)
        acc = buffer[0]
        for s in range(1, buffer.shape[0]):
            acc = acc + buffer[s]
        return acc

    def virt_stage(stage):
        if stage == 0:
            virt_c[core] = virt_feat[...]
            virt_exchange("vc", virt_c, core, 0, [(dom, mate)])
        elif stage == 1:
            virt_y[y] = virt_sum("vc", virt_c)
            virt_exchange(
                "vy", virt_y, y, 1, [(dom, y_peer(s) * 2 + core) for s in range(1, ny)]
            )
        elif stage == 2:
            virt_x[x] = virt_sum("vy", virt_y)
            virt_exchange(
                "vx", virt_x, x, ny, [(x_peer(s) * nz + z, row) for s in range(1, nx)]
            )
        elif stage == 3:
            virt_z[z] = virt_sum("vx", virt_x)
            virt_exchange(
                "vz", virt_z, z, ny + nx - 1, [(x * nz + z_peer(s), row) for s in range(1, nz)]
            )
        elif stage == 4:
            virt_total[...] = virt_sum("vz", virt_z)

    stages = [stage_c, stage_y, stage_x, stage_z, stage_all_x, stage_all_y, stage_all_c]

    put(0, contract(out_b, out_grad[...], 1, 0).astype(BF16))
    put(1, contract(ext_t[:, TILE:], dq_b, 1, 1).astype(BF16))
    stage_c(0)
    virt_hi = virt_t.astype(BF16)
    virt_lo = (virt_t - virt_hi.astype(F32)).astype(BF16)
    kv_sum = (
        contract(ext_t[...], kv_grad[...].astype(BF16), 1, 1)
        + contract(edge_x[...], edge_grad[...], 1, 1)
        + contract(virt_b, virt_hi[:, 0:VROWS], 0, 1)
        + contract(virt_b, virt_lo[:, 0:VROWS], 0, 1)
    ).astype(BF16)
    put(2, kv_sum[:, 0:width])
    put(3, kv_sum[:, width:])
    stage_c(1)
    stage_c(2)
    virt_feat[...] = (
        contract(virt_hi, w_keyval[...], 0, 1) + contract(virt_lo, w_keyval[...], 0, 1)
    )[0:8]
    virt_stage(0)
    halo_feat[...] = contract(kv_grad[:, 0:TILE].astype(BF16), w_keyval[...], 0, 1).astype(BF16)
    halo_return = remote(
        halo_feat,
        halo_back,
        sems_a.at[0],
        sems_a.at[1],
        dom,
        lax.rem(row + n_rows - 1, n_rows),
    )
    halo_return.start()
    edge_feat[...] = contract(w_keyval[...], edge_grad[...], 1, 0).astype(BF16)
    last = chunks - 1
    for stage, ch in wave_order([0.0] + [1.5] * last):
        if stage > 0:
            stages[stage](ch)
        if ch == last and 1 <= stage <= 4:
            virt_stage(stage)
        if (stage, ch) == (1, last):
            for g in range(groups // 2):
                slot_sums(g)
                slot_return(g)
            for g in range(groups // 2, groups):
                slot_sums(g)
            slots_back[dom] = slot_feat[0]
            grad_t = contract(w_query[...], dq_b, 1, 0) + contract(
                w_keyval[...], kv_grad[:, TILE:].astype(BF16), 1, 0
            )
            grad_feat[...] = grad_t.T
        if (stage, ch) == (3, last):
            for g in range(groups // 2, groups):
                slot_return(g)
    halo_return.wait()
    lax.fori_loop(1, n_dom, back_wait, 0)
    summed = grad_feat[...] + contract(
        picker[...], slots_back[...].reshape(slot_count, width), 1, 0
    )
    grad_feat[0 : row_count - TILE] = summed[0 : row_count - TILE]
    grad_feat[row_count - TILE :] = summed[row_count - TILE :] + halo_back[...].astype(F32)
    for ch in range(chunks):
        finish(("gc", ch))


def finish_kernel(
    factor, total, virt_in, feat_in, gq, gkv, go, gv, gf, gq_v, gkv_v, go_v, gv_v, sems
):
    width = gq_v.shape[1]
    copies = [
        pltpu.make_async_copy(src, dst, sems.at[i])
        for i, (src, dst) in enumerate(
            [(feat_in, gf), (go_v, go), (gq_v, gq), (gkv_v, gkv), (gv_v, gv)]
        )
    ]
    copies[0].start()
    go_v[...] = total[0:width].astype(F32) * factor
    copies[1].start()
    gq_v[...] = total[width : 2 * width].astype(F32) * factor
    copies[2].start()
    gkv_v[:, 0:width] = total[2 * width : 3 * width].astype(F32) * factor
    gkv_v[:, width:] = total[3 * width :].astype(F32) * factor
    copies[3].start()
    gv_v[...] = virt_in[0 : gv_v.shape[0]] * factor
    copies[4].start()
    for copy in copies:
        copy.wait()


def shards(sizes, features, out_grad, w_query, w_keyval, w_out, virtual, local_nbr, expander, send_rows):
    nx, nz, ny = sizes
    n_dom, n_rows = nx * nz, 2 * ny
    rows, width = features.shape
    per_peer = send_rows.shape[1]
    slots = n_dom * per_peer
    dma, shape = pltpu.SemaphoreType.DMA, jax.ShapeDtypeStruct
    chunks = 3
    height = 4 * width // chunks
    half = height // 2
    quarter = half // ny
    piece = quarter // nx
    tiles = rows // TILE
    grad_feat, total, virt_total = pl.pallas_call(
        functools.partial(whole_kernel, sizes),
        name="whole",
        out_shape=(
            shape((rows, width), F32),
            shape((chunks, height, width), BF16),
            shape((8, width), F32),
        ),
        in_specs=[pl.BlockSpec(memory_space=pl.ANY)] * 5 + [VMEM] * 4,
        out_specs=(VMEM,) * 3,
        scratch_shapes=[
            pltpu.VMEM((rows, width), BF16),
            pltpu.VMEM((rows, width), BF16),
            pltpu.VMEM((width, width), BF16),
            pltpu.VMEM((width, 2 * width), BF16),
            pltpu.VMEM((width, width), BF16),
            pltpu.VMEM((rows, slots), BF16),
            pltpu.VMEM((n_dom, per_peer, width), BF16),
            pltpu.VMEM((n_dom, per_peer, width), BF16),
            pltpu.VMEM((TILE, width), BF16),
            pltpu.VMEM((VROWS, width), F32),
            pltpu.VMEM((2 * width, width), BF16),
            pltpu.VMEM((width, rows + TILE), BF16),
            pltpu.VMEM((width, 4 * rows), BF16),
            pltpu.VMEM((width, 4 * rows), F32),
            pltpu.VMEM((width, rows), BF16),
            pltpu.VMEM((width, rows), BF16),
            pltpu.VMEM((2 * width, rows + TILE), BF16),
            pltpu.VMEM((slots, 4 * rows), BF16),
            pltpu.VMEM((2 * TILE, rows), F32),
            pltpu.VMEM((2 * width, 4 * rows), F32),
            pltpu.VMEM((HEADS, tiles, 2 * TILE, TILE), F32),
            pltpu.VMEM((HEADS, tiles, 2 * TILE, TILE), F32),
            pltpu.VMEM((HEADS, rows), F32),
            pltpu.VMEM((HEADS, rows), F32),
            pltpu.VMEM((HEADS, rows), F32),
            pltpu.VMEM((2 * width, rows + TILE), F32),
            pltpu.VMEM((width, rows), F32),
            pltpu.VMEM((width, rows), F32),
            pltpu.VMEM((2 * width, 4 * rows), BF16),
            pltpu.VMEM((width, 4 * rows), BF16),
            pltpu.VMEM((n_dom, per_peer, width), BF16),
            pltpu.VMEM((TILE, width), BF16),
            pltpu.VMEM((n_dom, per_peer, width), BF16),
            pltpu.VMEM((TILE, width), BF16),
            pltpu.VMEM((chunks, height, width), BF16),
            pltpu.VMEM((chunks, half, width), BF16),
            pltpu.VMEM((chunks, half, width), BF16),
            pltpu.VMEM((chunks, ny - 1, quarter, width), BF16),
            pltpu.VMEM((chunks, quarter, width), BF16),
            pltpu.VMEM((chunks, nx - 1, piece, width), BF16),
            pltpu.VMEM((chunks, piece, width), BF16),
            pltpu.VMEM((chunks, nz, piece, width), BF16),
            pltpu.VMEM((chunks, quarter, width), BF16),
            pltpu.VMEM((chunks, half, width), BF16),
            pltpu.VMEM((8, width), F32),
            pltpu.VMEM((2, 8, width), F32),
            pltpu.VMEM((ny, 8, width), F32),
            pltpu.VMEM((nx, 8, width), F32),
            pltpu.VMEM((nz, 8, width), F32),
            dma((5,)),
            dma((2, n_dom)),
            dma((2, n_dom)),
            dma((2,)),
            dma((2,)),
            dma((2, chunks)),
            dma((2, chunks, ny)),
            dma((2, chunks, nx)),
            dma((2, chunks, nz)),
            dma((2, chunks, nx)),
            dma((2, chunks, ny)),
            dma((2, chunks)),
            dma((2, nx + ny + nz)),
        ],
        compiler_params=pltpu.CompilerParams(
            collective_id=0, has_side_effects=True, vmem_limit_bytes=60 << 20
        ),
    )(
        features,
        out_grad,
        w_query,
        w_keyval,
        w_out,
        virtual,
        local_nbr.T,
        expander.T,
        send_rows,
    )

    anywhere = pl.BlockSpec(memory_space=pl.ANY)
    gq, gkv, go, gv, gf = pl.pallas_call(
        functools.partial(finish_kernel, (rows * n_dom * n_rows) ** (-0.5)),
        name="finish",
        out_shape=(
            shape((width, width), F32),
            shape((width, 2 * width), F32),
            shape((width, width), F32),
            shape((virtual.shape[0], width), F32),
            shape((rows, width), F32),
        ),
        in_specs=[VMEM] * 3,
        out_specs=(anywhere,) * 5,
        scratch_shapes=[
            pltpu.VMEM((width, width), F32),
            pltpu.VMEM((width, 2 * width), F32),
            pltpu.VMEM((width, width), F32),
            pltpu.VMEM((virtual.shape[0], width), F32),
            dma((5,)),
        ],
    )(total.reshape(chunks * height, width), virt_total, grad_feat)
    return gf, gq, gkv, go, gv


def solution(mesh):
    n_dom, n_rows = mesh.shape["dom"], mesh.shape["rows"]
    nx = 4 if n_dom % 32 == 0 else 2
    sizes = (nx, n_dom // nx, n_rows // 2)
    across = P(("dom", "rows"), None)
    placed = (across, across, P(), P(), P(), P(), across, across, across)
    return jax.shard_map(
        functools.partial(shards, sizes),
        mesh=mesh,
        in_specs=placed,
        out_specs=(across, P(), P(), P(), P()),
        check_vma=False,
    )
```

```python
import functools
import heapq
import math

import jax
import jax.numpy as jnp
from jax import lax
from jax.experimental import pallas as pl
from jax.experimental.pallas import tpu as pltpu
from jax.sharding import PartitionSpec as P

HEADS = 8
TILE = 128
LANES = 128
VROWS = 16
NEGATIVE_FILL = -1e30

F32 = jnp.float32
BF16 = jnp.bfloat16
VMEM = pl.BlockSpec(memory_space=pltpu.VMEM)


def contract(left, right, left_dim, right_dim):
    return lax.dot_general(
        left, right, (((left_dim,), (right_dim,)), ((), ())), preferred_element_type=F32
    )


def remote(src, dst, send_sem, recv_sem, dom, row):
    return pltpu.make_async_remote_copy(
        src_ref=src,
        dst_ref=dst,
        send_sem=send_sem,
        recv_sem=recv_sem,
        device_id=(dom, row),
        device_id_type=pl.DeviceIdType.MESH,
    )


def greet(n_dom, n_rows):
    dom, row = lax.axis_index("dom"), lax.axis_index("rows")
    barrier = pltpu.get_barrier_semaphore()

    def dom_peer(step, carry):
        pl.semaphore_signal(
            barrier,
            inc=1,
            device_id=(lax.rem(dom + step, n_dom), row),
            device_id_type=pl.DeviceIdType.MESH,
        )
        return carry

    def row_peer(step, carry):
        pl.semaphore_signal(
            barrier,
            inc=1,
            device_id=(dom, lax.rem(row + step, n_rows)),
            device_id_type=pl.DeviceIdType.MESH,
        )
        return carry

    lax.fori_loop(1, n_dom, dom_peer, 0)
    lax.fori_loop(1, n_rows, row_peer, 0)
    return barrier, n_dom + n_rows - 2


def wave_order(first):
    chunks = len(first)
    track = ["c", "y", "x", "z", "y", "c"]
    load = [1.5, 6.5, 2.0, 6.5, 6.5, 1.5]
    lag = [1.0, 2.5, 2.5, 4.0, 4.0, 1.0]
    free = {name: 0.0 for name in track}
    ready = [(start, ch, 0) for ch, start in enumerate(first)]
    heapq.heapify(ready)
    order = []
    while ready:
        now, ch, stage = heapq.heappop(ready)
        order.append((stage, ch))
        if stage + 1 < len(track):
            begin = max(now, free[track[stage]])
            free[track[stage]] = begin + load[stage] / chunks
            heapq.heappush(ready, (free[track[stage]] + lag[stage], ch, stage + 1))
    return order


def whole_kernel(
    sizes,
    feat_in,
    out_grad_in,
    w_query_in,
    w_keyval_in,
    w_out_in,
    virt,
    local_nbr,
    expander,
    send_rows,
    grad_feat,
    total,
    virt_total,
    feat,
    out_grad,
    w_query,
    w_keyval,
    w_out,
    picker,
    picked,
    slots,
    halo,
    virt_pad,
    wkv_t,
    ext_t,
    edge_x,
    edge_x_sum,
    q_t,
    d_t,
    kv_t,
    named,
    bias,
    edge_kv,
    weight_e,
    weight_dp,
    rows_s,
    rows_f,
    rows_d,
    kv_grad,
    out_t,
    dq_t,
    edge_grad,
    edge_feat,
    slot_feat,
    halo_feat,
    slots_back,
    halo_back,
    sums,
    got_c,
    sum_c,
    got_y,
    sum_y,
    got_x,
    sum_x,
    got_z,
    all_p,
    virt_feat,
    virt_c,
    virt_y,
    virt_x,
    virt_z,
    sems_in,
    sems_s,
    sems_g,
    sems_a,
    sems_h,
    sems_c,
    sems_y,
    sems_x,
    sems_z,
    sems_gp,
    sems_gc,
    sems_v,
):
    nx, nz, ny = sizes
    n_dom, n_rows = nx * nz, 2 * ny
    dom, row = lax.axis_index("dom"), lax.axis_index("rows")
    x, z = dom // nz, lax.rem(dom, nz)
    y, core = row // 2, lax.rem(row, 2)
    mate = row + 1 - 2 * core
    row_count, width = feat.shape
    per_peer = send_rows.shape[1]
    slot_count = n_dom * per_peer
    head_dim = width // HEADS
    degree = expander.shape[0]
    scale = 1.0 / math.sqrt(head_dim)
    tiles = row_count // TILE
    bits = per_peer.bit_length() - 1
    groups = nx
    per_group = nz
    span = per_group * per_peer

    def distance(offset, size):
        return min(offset, size - offset)

    far_groups = sorted(range(groups), key=lambda dx: -distance(dx, nx))
    far_first = sorted(
        [(dx, dz) for dx in range(nx) for dz in range(nz)][1:],
        key=lambda offset: -distance(offset[0], nx) - distance(offset[1], nz),
    )

    barrier, arrivals = greet(n_dom, n_rows)
    loads = [
        pltpu.make_async_copy(src, dst, sems_in.at[i])
        for i, (src, dst) in enumerate(
            [
                (feat_in, feat),
                (w_keyval_in, w_keyval),
                (w_query_in, w_query),
                (w_out_in, w_out),
                (out_grad_in, out_grad),
            ]
        )
    ]
    for load in loads:
        load.start()

    spot = lax.broadcasted_iota(jnp.int32, (per_peer, slot_count), 1)
    entry = lax.broadcasted_iota(jnp.int32, (per_peer, slot_count), 0)
    spread = (jnp.bitwise_and(spot, per_peer - 1) == entry).astype(F32).astype(BF16)
    listed = contract(send_rows[...].astype(F32).astype(BF16), spread, 1, 0)
    owner = lax.broadcasted_iota(jnp.int32, (n_dom, slot_count), 0)
    column = lax.broadcasted_iota(jnp.int32, (n_dom, slot_count), 1)
    mine = jnp.right_shift(column, bits) == owner
    send_flat = jnp.sum(jnp.where(mine, listed, 0.0), axis=0, keepdims=True).astype(jnp.int32)
    rows_at = lax.broadcasted_iota(jnp.int32, (row_count, slot_count), 0)
    picker[...] = (rows_at == send_flat).astype(F32).astype(BF16)
    loads[0].wait()
    picked[...] = contract(picker[...], feat[...], 0, 0).astype(BF16).reshape(picked.shape)

    pl.semaphore_wait(barrier, arrivals)

    halo_copy = remote(
        feat.at[pl.ds(row_count - TILE, TILE)],
        halo,
        sems_h.at[0],
        sems_h.at[1],
        dom,
        lax.rem(row + 1, n_rows),
    )
    halo_copy.start()

    def spread_copy(dx, dz):
        peer = lax.rem(x + dx, nx) * nz + lax.rem(z + dz, nz)
        step = dx * nz + dz
        return remote(
            picked.at[peer], slots.at[step], sems_s.at[0, step], sems_s.at[1, step], peer, row
        )

    for dx, dz in far_first:
        spread_copy(dx, dz).start()
    slots[0] = picked[dom]

    for load in loads[1:]:
        load.wait()
    wkv_t[...] = w_keyval[...].T
    ext_t[:, TILE:] = feat[...].T
    q_t[...] = contract(w_query[...], ext_t[:, TILE:], 0, 0).astype(BF16)
    d_t[...] = contract(w_out[...], out_grad[...], 1, 1).astype(BF16)
    kv_t[:, TILE:] = contract(wkv_t[...], ext_t[:, TILE:], 1, 0).astype(BF16)
    virt_pad[...] = jnp.zeros_like(virt_pad)
    virt_pad[0 : virt.shape[0]] = virt[...].astype(F32)
    virt_b = virt_pad[...].astype(BF16)
    virt_kv = contract(wkv_t[...], virt_b, 1, 1).astype(BF16).astype(F32)

    positions = lax.broadcasted_iota(jnp.int32, (2 * TILE, row_count), 0)
    mask = positions == local_nbr[0:1, :]
    for place in range(1, local_nbr.shape[0]):
        mask = jnp.logical_or(mask, positions == local_nbr[place : place + 1, :])
    bias[...] = jnp.where(mask, 0.0, NEGATIVE_FILL)

    source = jnp.right_shift(expander[...], bits)
    away_x = jnp.bitwise_and(x - jnp.right_shift(source, nz.bit_length() - 1), nx - 1)
    away_z = jnp.bitwise_and(z - jnp.bitwise_and(source, nz - 1), nz - 1)
    away = away_x * nz + away_z
    slot_of = away * per_peer + jnp.bitwise_and(expander[...], per_peer - 1)
    slot_ids = lax.broadcasted_iota(jnp.int32, (slot_count, row_count), 0)
    for k in range(degree):
        named[:, k * row_count : (k + 1) * row_count] = (
            (slot_ids == slot_of[k : k + 1, :]).astype(F32).astype(BF16)
        )

    def per_head(product):
        return product.reshape(HEADS, head_dim, row_count).sum(axis=1)

    def virtual_edge(v):
        return jnp.broadcast_to(virt_kv[:, v : v + 1], (2 * width, row_count))

    virt_s, virt_dp = [], []
    for v in range(4):
        both = virtual_edge(v)
        virt_s.append(per_head(q_t[...].astype(F32) * both[0:width]) * scale)
        virt_dp.append(per_head(d_t[...].astype(F32) * both[width:]))

    halo_copy.wait()
    ext_t[:, 0:TILE] = halo[...].T
    kv_t[:, 0:TILE] = contract(wkv_t[...], ext_t[:, 0:TILE], 1, 0).astype(BF16)

    def places(h, t):
        own = slice(h * head_dim, (h + 1) * head_dim)
        val = slice(width + h * head_dim, width + (h + 1) * head_dim)
        return own, val, slice(t * TILE, (t + 1) * TILE), slice(t * TILE, (t + 2) * TILE)

    for h in range(HEADS):
        for t in range(tiles):
            own, val, here, window = places(h, t)
            s = contract(kv_t[own, window], q_t[own, here], 0, 0) * scale + bias[:, here]
            dp = contract(kv_t[val, window], d_t[own, here], 0, 0)
            peak = jnp.max(s, axis=0, keepdims=True)
            e = jnp.exp(s - peak)
            weight_e[h, t] = e
            weight_dp[h, t] = dp
            rows_s[h : h + 1, here] = peak
            rows_f[h : h + 1, here] = jnp.sum(e, axis=0, keepdims=True)
            rows_d[h : h + 1, here] = jnp.sum(e * dp, axis=0, keepdims=True)

    for turn, g in enumerate(far_groups):
        for dx, dz in far_first:
            if dx == g:
                spread_copy(dx, dz).wait()
        held = slice(g * span, (g + 1) * span)
        found = contract(
            slots[g * per_group : (g + 1) * per_group].reshape(span, width), named[held, :], 0, 0
        )
        if turn == 0:
            edge_x_sum[...] = found
        elif turn + 1 < groups:
            edge_x_sum[...] += found
        else:
            edge_x[...] = (edge_x_sum[...] + found).astype(BF16)
    edge_kv[...] = contract(wkv_t[...], edge_x[...], 1, 0).astype(BF16).astype(F32)

    q_wide = q_t[...].astype(F32)
    d_wide = d_t[...].astype(F32)
    cols = [slice(k * row_count, (k + 1) * row_count) for k in range(degree)]
    edge_s = [per_head(q_wide * edge_kv[0:width, c]) * scale for c in cols] + virt_s
    edge_dp = [per_head(d_wide * edge_kv[width:, c]) for c in cols] + virt_dp
    peak_loc = rows_s[...]
    peak = peak_loc
    for s in edge_s:
        peak = jnp.maximum(peak, s)
    shrink = jnp.exp(peak_loc - peak)
    edge_e = [jnp.exp(s - peak) for s in edge_s]
    norm = rows_f[...] * shrink
    for e in edge_e:
        norm = norm + e
    inverse = 1.0 / norm
    edge_p = [e * inverse for e in edge_e]
    share = shrink * inverse
    delta = rows_d[...] * share
    for p, dp in zip(edge_p, edge_dp):
        delta = delta + p * dp
    rows_f[...] = share
    rows_d[...] = delta
    edge_ds = [
        (p * (dp - delta) * scale).astype(BF16).astype(F32) for p, dp in zip(edge_p, edge_dp)
    ]
    edge_p = [p.astype(BF16).astype(F32) for p in edge_p]

    def widen(values):
        return jnp.broadcast_to(values[:, None, :], (HEADS, head_dim, row_count)).reshape(
            width, row_count
        )

    out_sum = jnp.zeros((width, row_count), F32)
    dq_sum = jnp.zeros((width, row_count), F32)
    for k in range(degree):
        pk, dsk = widen(edge_p[k]), widen(edge_ds[k])
        out_sum = out_sum + pk * edge_kv[width:, cols[k]]
        dq_sum = dq_sum + dsk * edge_kv[0:width, cols[k]]
        edge_grad[0:width, cols[k]] = (dsk * q_wide).astype(BF16)
        edge_grad[width:, cols[k]] = (pk * d_wide).astype(BF16)
    out_t[...] = out_sum
    dq_t[...] = dq_sum

    def back_copy(dx, dz):
        peer = lax.rem(x - dx + nx, nx) * nz + lax.rem(z - dz + nz, nz)
        step = dx * nz + dz
        return remote(
            slot_feat.at[step],
            slots_back.at[dom],
            sems_g.at[0, step],
            sems_g.at[1, step],
            peer,
            row,
        )

    def slot_sums(g):
        held = slice(g * span, (g + 1) * span)
        slot_feat[g * per_group : (g + 1) * per_group] = (
            contract(named[held, :], edge_feat[...], 1, 1)
            .astype(BF16)
            .reshape(per_group, per_peer, width)
        )

    def slot_return(g):
        for dx, dz in far_first:
            if dx == g:
                back_copy(dx, dz).start()

    edge_feat[...] = contract(w_keyval[...], edge_grad[...], 1, 0).astype(BF16)
    for g in far_groups[: groups // 2]:
        slot_sums(g)
        slot_return(g)
    kv_grad[...] = jnp.zeros_like(kv_grad)
    for h in range(HEADS):
        for t in range(tiles):
            own, val, here, window = places(h, t)
            p = weight_e[h, t] * rows_f[h : h + 1, here]
            ds = (p * (weight_dp[h, t] - rows_d[h : h + 1, here]) * scale).astype(BF16)
            pb = p.astype(BF16)
            out_t[own, here] += contract(kv_t[val, window], pb, 1, 0)
            dq_t[own, here] += contract(kv_t[own, window], ds, 1, 0)
            kv_grad[own, window] += contract(q_t[own, here], ds, 1, 1)
            kv_grad[val, window] += contract(d_t[own, here], pb, 1, 1)

    lane = lax.broadcasted_iota(jnp.int32, (2 * width, LANES), 1)
    virt_t = jnp.zeros((2 * width, LANES), F32)
    out_sum = out_t[...]
    dq_sum = dq_t[...]
    for v in range(4):
        pk, dsk = widen(edge_p[degree + v]), widen(edge_ds[degree + v])
        both = virtual_edge(v)
        out_sum = out_sum + pk * both[width:]
        dq_sum = dq_sum + dsk * both[0:width]
        to_both = jnp.concatenate(
            [
                jnp.sum(dsk * q_wide, axis=1, keepdims=True),
                jnp.sum(pk * d_wide, axis=1, keepdims=True),
            ],
            axis=0,
        )
        virt_t = jnp.where(lane == v, to_both, virt_t)
    out_b = out_sum.astype(BF16)
    dq_b = dq_sum.astype(BF16)

    chunks, height = sums.shape[0], sums.shape[1]
    half, quarter, piece = height // 2, height // 2 // ny, height // 2 // ny // nx

    def put(block_index, value):
        first = block_index * width
        while value.shape[0]:
            ch, at = divmod(first, height)
            count = min(height - at, value.shape[0])
            sums[ch, at : at + count] = value[0:count]
            value = value[count:]
            first += count

    def block(index, size):
        return pl.ds(pl.multiple_of(index * size, 16), size)

    def y_peer(step):
        return lax.rem(y + step, ny)

    def x_peer(step):
        return lax.rem(x + step, nx)

    def z_peer(step):
        return lax.rem(z + step, nz)

    started = {}

    def start(key, copies):
        for copy in copies:
            copy.start()
        started[key] = copies

    def finish(key):
        for copy in started.pop(key):
            copy.wait()

    def stage_c(ch):
        start(
            ("c", ch),
            [
                remote(
                    sums.at[ch, block(1 - core, half)],
                    got_c.at[ch],
                    sems_c.at[0, ch],
                    sems_c.at[1, ch],
                    dom,
                    mate,
                )
            ],
        )

    plane = [(dx, dy) for dx in range(nx) for dy in range(ny)][1:]

    def plane_peer(dx, dy):
        return x_peer(dx) * nz + z, y_peer(dy) * 2 + core

    def stage_y(ch):
        finish(("c", ch))
        sum_c[ch] = (sums[ch, block(core, half)].astype(F32) + got_c[ch].astype(F32)).astype(BF16)
        start(
            ("y", ch),
            [
                remote(
                    sum_c.at[ch, block(y_peer(s), quarter)],
                    got_y.at[ch, s - 1],
                    sems_y.at[0, ch, s],
                    sems_y.at[1, ch, s],
                    dom,
                    y_peer(s) * 2 + core,
                )
                for s in range(1, ny)
            ],
        )

    def stage_x(ch):
        finish(("y", ch))
        acc = sum_c[ch, block(y, quarter)].astype(F32)
        for s in range(ny - 1):
            acc = acc + got_y[ch, s].astype(F32)
        sum_y[ch] = acc.astype(BF16)
        start(
            ("x", ch),
            [
                remote(
                    sum_y.at[ch, block(x_peer(s), piece)],
                    got_x.at[ch, s - 1],
                    sems_x.at[0, ch, s],
                    sems_x.at[1, ch, s],
                    x_peer(s) * nz + z,
                    row,
                )
                for s in range(1, nx)
            ],
        )

    def stage_z(ch):
        finish(("x", ch))
        acc = sum_y[ch, block(x, piece)].astype(F32)
        for s in range(nx - 1):
            acc = acc + got_x[ch, s].astype(F32)
        sum_x[ch] = acc.astype(BF16)
        start(
            ("z", ch),
            [
                remote(
                    sum_x.at[ch],
                    got_z.at[ch, z],
                    sems_z.at[0, ch, s],
                    sems_z.at[1, ch, s],
                    x * nz + z_peer(s),
                    row,
                )
                for s in range(1, nz)
            ],
        )
        got_z[ch, z] = acc.astype(BF16)

    def stage_all_plane(ch):
        finish(("z", ch))
        acc = got_z[ch, 0].astype(F32)
        for s in range(1, nz):
            acc = acc + got_z[ch, s].astype(F32)
        mine = block(y * nx + x, piece)
        all_p[ch, mine] = acc.astype(BF16)
        start(
            ("gp", ch),
            [
                remote(
                    all_p.at[ch, mine],
                    all_p.at[ch, mine],
                    sems_gp.at[0, ch, i],
                    sems_gp.at[1, ch, i],
                    *plane_peer(dx, dy),
                )
                for i, (dx, dy) in enumerate(plane)
            ],
        )

    def stage_all_c(ch):
        finish(("gp", ch))
        start(
            ("gc", ch),
            [
                remote(
                    all_p.at[ch],
                    total.at[ch, block(core, half)],
                    sems_gc.at[0, ch],
                    sems_gc.at[1, ch],
                    dom,
                    mate,
                )
            ],
        )
        total[ch, block(core, half)] = all_p[ch]

    def virt_exchange(key, buffer, index, first, peers):
        start(
            key,
            [
                remote(
                    buffer.at[index],
                    buffer.at[index],
                    sems_v.at[0, first + s],
                    sems_v.at[1, first + s],
                    to_dom,
                    to_row,
                )
                for s, (to_dom, to_row) in enumerate(peers)
            ],
        )

    def virt_sum(key, buffer):
        finish(key)
        acc = buffer[0]
        for s in range(1, buffer.shape[0]):
            acc = acc + buffer[s]
        return acc

    def virt_stage(stage):
        if stage == 0:
            virt_c[core] = virt_feat[...]
            virt_exchange("vc", virt_c, core, 0, [(dom, mate)])
        elif stage == 1:
            virt_y[y] = virt_sum("vc", virt_c)
            virt_exchange(
                "vy", virt_y, y, 1, [(dom, y_peer(s) * 2 + core) for s in range(1, ny)]
            )
        elif stage == 2:
            virt_x[x] = virt_sum("vy", virt_y)
            virt_exchange(
                "vx", virt_x, x, ny, [(x_peer(s) * nz + z, row) for s in range(1, nx)]
            )
        elif stage == 3:
            virt_z[z] = virt_sum("vx", virt_x)
            virt_exchange(
                "vz", virt_z, z, ny + nx - 1, [(x * nz + z_peer(s), row) for s in range(1, nz)]
            )
        elif stage == 4:
            virt_total[...] = virt_sum("vz", virt_z)

    stages = [stage_c, stage_y, stage_x, stage_z, stage_all_plane, stage_all_c]

    put(0, contract(out_b, out_grad[...], 1, 0).astype(BF16))
    put(1, contract(ext_t[:, TILE:], dq_b, 1, 1).astype(BF16))
    stage_c(0)
    virt_hi = virt_t.astype(BF16)
    virt_lo = (virt_t - virt_hi.astype(F32)).astype(BF16)
    kv_sum = (
        contract(ext_t[...], kv_grad[...].astype(BF16), 1, 1)
        + contract(edge_x[...], edge_grad[...], 1, 1)
        + contract(virt_b, virt_hi[:, 0:VROWS], 0, 1)
        + contract(virt_b, virt_lo[:, 0:VROWS], 0, 1)
    ).astype(BF16)
    put(2, kv_sum[:, 0:width])
    put(3, kv_sum[:, width:])
    stage_c(1)
    stage_c(2)
    last = chunks - 1
    virt_at = {(2, last): 1, (3, last): 2, (4, last): 3}
    for stage, ch in wave_order([0.0] + [1.5] * last):
        if stage > 0:
            stages[stage](ch)
        if (stage, ch) in virt_at:
            virt_stage(virt_at[(stage, ch)])
        if (stage, ch) == (1, last):
            virt_feat[...] = (
                contract(virt_hi, w_keyval[...], 0, 1) + contract(virt_lo, w_keyval[...], 0, 1)
            )[0:8]
            virt_stage(0)
            halo_feat[...] = contract(
                kv_grad[:, 0:TILE].astype(BF16), w_keyval[...], 0, 1
            ).astype(BF16)
            halo_return = remote(
                halo_feat,
                halo_back,
                sems_a.at[0],
                sems_a.at[1],
                dom,
                lax.rem(row + n_rows - 1, n_rows),
            )
            halo_return.start()
        if (stage, ch) == (3, last):
            for g in far_groups[groups // 2 :]:
                slot_sums(g)
                slot_return(g)
            slots_back[dom] = slot_feat[0]
            grad_t = contract(w_query[...], dq_b, 1, 0) + contract(
                w_keyval[...], kv_grad[:, TILE:].astype(BF16), 1, 0
            )
            grad_feat[...] = grad_t.T
    halo_return.wait()
    for dx, dz in far_first:
        back_copy(dx, dz).wait()
    summed = grad_feat[...] + contract(
        picker[...], slots_back[...].reshape(slot_count, width), 1, 0
    )
    grad_feat[0 : row_count - TILE] = summed[0 : row_count - TILE]
    grad_feat[row_count - TILE :] = summed[row_count - TILE :] + halo_back[...].astype(F32)
    virt_stage(4)
    for ch in range(chunks):
        finish(("gc", ch))


def finish_kernel(
    factor, total, virt_in, feat_in, gq, gkv, go, gv, gf, gq_v, gkv_v, go_v, gv_v, sems
):
    width = gq_v.shape[1]
    copies = [
        pltpu.make_async_copy(src, dst, sems.at[i])
        for i, (src, dst) in enumerate(
            [(feat_in, gf), (go_v, go), (gq_v, gq), (gkv_v, gkv), (gv_v, gv)]
        )
    ]
    copies[0].start()
    go_v[...] = total[0:width].astype(F32) * factor
    copies[1].start()
    gq_v[...] = total[width : 2 * width].astype(F32) * factor
    copies[2].start()
    gkv_v[:, 0:width] = total[2 * width : 3 * width].astype(F32) * factor
    gkv_v[:, width:] = total[3 * width :].astype(F32) * factor
    copies[3].start()
    gv_v[...] = virt_in[0 : gv_v.shape[0]] * factor
    copies[4].start()
    for copy in copies:
        copy.wait()


def shards(sizes, features, out_grad, w_query, w_keyval, w_out, virtual, local_nbr, expander, send_rows):
    nx, nz, ny = sizes
    n_dom, n_rows = nx * nz, 2 * ny
    rows, width = features.shape
    per_peer = send_rows.shape[1]
    slots = n_dom * per_peer
    dma, shape = pltpu.SemaphoreType.DMA, jax.ShapeDtypeStruct
    chunks = 3
    height = 4 * width // chunks
    half = height // 2
    quarter = half // ny
    piece = quarter // nx
    tiles = rows // TILE
    grad_feat, total, virt_total = pl.pallas_call(
        functools.partial(whole_kernel, sizes),
        name="whole",
        out_shape=(
            shape((rows, width), F32),
            shape((chunks, height, width), BF16),
            shape((8, width), F32),
        ),
        in_specs=[pl.BlockSpec(memory_space=pl.ANY)] * 5 + [VMEM] * 4,
        out_specs=(VMEM,) * 3,
        scratch_shapes=[
            pltpu.VMEM((rows, width), BF16),
            pltpu.VMEM((rows, width), BF16),
            pltpu.VMEM((width, width), BF16),
            pltpu.VMEM((width, 2 * width), BF16),
            pltpu.VMEM((width, width), BF16),
            pltpu.VMEM((rows, slots), BF16),
            pltpu.VMEM((n_dom, per_peer, width), BF16),
            pltpu.VMEM((n_dom, per_peer, width), BF16),
            pltpu.VMEM((TILE, width), BF16),
            pltpu.VMEM((VROWS, width), F32),
            pltpu.VMEM((2 * width, width), BF16),
            pltpu.VMEM((width, rows + TILE), BF16),
            pltpu.VMEM((width, 4 * rows), BF16),
            pltpu.VMEM((width, 4 * rows), F32),
            pltpu.VMEM((width, rows), BF16),
            pltpu.VMEM((width, rows), BF16),
            pltpu.VMEM((2 * width, rows + TILE), BF16),
            pltpu.VMEM((slots, 4 * rows), BF16),
            pltpu.VMEM((2 * TILE, rows), F32),
            pltpu.VMEM((2 * width, 4 * rows), F32),
            pltpu.VMEM((HEADS, tiles, 2 * TILE, TILE), F32),
            pltpu.VMEM((HEADS, tiles, 2 * TILE, TILE), F32),
            pltpu.VMEM((HEADS, rows), F32),
            pltpu.VMEM((HEADS, rows), F32),
            pltpu.VMEM((HEADS, rows), F32),
            pltpu.VMEM((2 * width, rows + TILE), F32),
            pltpu.VMEM((width, rows), F32),
            pltpu.VMEM((width, rows), F32),
            pltpu.VMEM((2 * width, 4 * rows), BF16),
            pltpu.VMEM((width, 4 * rows), BF16),
            pltpu.VMEM((n_dom, per_peer, width), BF16),
            pltpu.VMEM((TILE, width), BF16),
            pltpu.VMEM((n_dom, per_peer, width), BF16),
            pltpu.VMEM((TILE, width), BF16),
            pltpu.VMEM((chunks, height, width), BF16),
            pltpu.VMEM((chunks, half, width), BF16),
            pltpu.VMEM((chunks, half, width), BF16),
            pltpu.VMEM((chunks, ny - 1, quarter, width), BF16),
            pltpu.VMEM((chunks, quarter, width), BF16),
            pltpu.VMEM((chunks, nx - 1, piece, width), BF16),
            pltpu.VMEM((chunks, piece, width), BF16),
            pltpu.VMEM((chunks, nz, piece, width), BF16),
            pltpu.VMEM((chunks, half, width), BF16),
            pltpu.VMEM((8, width), F32),
            pltpu.VMEM((2, 8, width), F32),
            pltpu.VMEM((ny, 8, width), F32),
            pltpu.VMEM((nx, 8, width), F32),
            pltpu.VMEM((nz, 8, width), F32),
            dma((5,)),
            dma((2, n_dom)),
            dma((2, n_dom)),
            dma((2,)),
            dma((2,)),
            dma((2, chunks)),
            dma((2, chunks, ny)),
            dma((2, chunks, nx)),
            dma((2, chunks, nz)),
            dma((2, chunks, nx * ny)),
            dma((2, chunks)),
            dma((2, nx + ny + nz)),
        ],
        compiler_params=pltpu.CompilerParams(
            collective_id=0, has_side_effects=True, vmem_limit_bytes=60 << 20
        ),
    )(
        features,
        out_grad,
        w_query,
        w_keyval,
        w_out,
        virtual,
        local_nbr.T,
        expander.T,
        send_rows,
    )

    anywhere = pl.BlockSpec(memory_space=pl.ANY)
    gq, gkv, go, gv, gf = pl.pallas_call(
        functools.partial(finish_kernel, (rows * n_dom * n_rows) ** (-0.5)),
        name="finish",
        out_shape=(
            shape((width, width), F32),
            shape((width, 2 * width), F32),
            shape((width, width), F32),
            shape((virtual.shape[0], width), F32),
            shape((rows, width), F32),
        ),
        in_specs=[VMEM] * 3,
        out_specs=(anywhere,) * 5,
        scratch_shapes=[
            pltpu.VMEM((width, width), F32),
            pltpu.VMEM((width, 2 * width), F32),
            pltpu.VMEM((width, width), F32),
            pltpu.VMEM((virtual.shape[0], width), F32),
            dma((5,)),
        ],
    )(total.reshape(chunks * height, width), virt_total, grad_feat)
    return gf, gq, gkv, go, gv


def solution(mesh):
    n_dom, n_rows = mesh.shape["dom"], mesh.shape["rows"]
    nx = 4 if n_dom % 32 == 0 else 2
    sizes = (nx, n_dom // nx, n_rows // 2)
    across = P(("dom", "rows"), None)
    placed = (across, across, P(), P(), P(), P(), across, across, across)
    return jax.shard_map(
        functools.partial(shards, sizes),
        mesh=mesh,
        in_specs=placed,
        out_specs=(across, P(), P(), P(), P()),
        check_vma=False,
    )
```
